32 devices in a mesh: gx: 4 (over z), gy: 4 (over x, core), gz: 2 (over y).
Axes of the slice: x: 2, y: 2, z: 4, core: 2. Of those that a mesh axis runs over, the one named last changes fastest.
Arguments:
- offsets: float32 [3, 8, 16, 8, 256], P(None, 'gx', 'gy', 'gz'), may hold values from 0 to 1
- charges: float32 [8, 16, 8, 256], P('gx', 'gy', 'gz'), may hold values from -0.6 to 0.6
- counts: int32 [8, 16, 8], P('gx', 'gy', 'gz'), may hold values from 1 to 256
- owned_cell: int32 [128], P(('gx', 'gy', 'gz')), may hold values from 0 to 127, each once
- list_sources: int32 [128, 189], P(('gx', 'gy', 'gz')), may hold values from 0 to 127
- list_ops: int32 [128, 189], P(('gx', 'gy', 'gz')), may hold values from 0 to 255
- m2m: float32 [8, 121, 121], replicated, may hold values from -0.1875 to 0.1875
- m2l: bfloat16 [121, 121, 256], replicated, may hold values from -0.0390625 to 0.0390625
- l2l: float32 [8, 121, 121], replicated, may hold values from -0.5 to 0.5
Outputs:
- potential: float32 [8, 16, 8, 256], P('gx', 'gy', 'gz')
The draws below stay inside these ranges and needn't reach their ends.
Inputs may be any that keep to these rules, and one draw needn't show every extreme that they name: `owned_cell`: a permutation of the parent cells.
All inputs are finite; a program needn't handle non-finite values.
Results may differ from the reference program's by a relative error of at most 0.0003.
Values may be sent and summed in bfloat16 or wider, within the bound.
No kernel may reach another device: no remote copies, remote signals or barrier semaphores. Data moves between devices by JAX's collectives and lax.ppermute only.
A program may use at most 64 MiB of HBM per device.

```python
import math
import jax
import jax.numpy as jnp
from jax import lax

SLOTS = 256
ORDER = 10
COEF = 121
OPS = 256
LIST = 189
NXL = 8
NYL = 16
NZL = 8
PARENTS = 128


def plant(entries, rng, low, largest):
    spot = [jax.random.randint(jax.random.fold_in(rng, axis), (), 0, length) for axis, length in enumerate(entries.shape)]
    main_axis = entries.shape.index(max(entries.shape))
    neighbour = spot[:main_axis] + [(spot[main_axis] + 1) % entries.shape[main_axis]] + spot[main_axis + 1:]
    return entries.at[tuple(spot)].set(low).at[tuple(neighbour)].set(largest)


def steps_of(rng, extent, cuts, smallest, top_value):
    def one(position, blocks):
        heights = jax.random.uniform(jax.random.fold_in(jax.random.fold_in(rng, 6), position), (blocks,), jnp.float32, smallest / len(cuts), top_value / len(cuts))
        return jnp.repeat(jnp.exp(heights), extent[position] // blocks).reshape((-1,) + (1,) * (len(extent) - position - 1))

    loudness = one(*cuts[0])
    for cut in cuts[1:]:
        loudness = loudness * one(*cut)
    return loudness


def centred(rng, dims, spread, bound, shards=(), kind=jnp.bfloat16):
    drawn = spread * jax.random.normal(rng, dims, jnp.float32)
    if shards:
        drawn = drawn * steps_of(rng, dims, shards, -0.22, 0.18)
    return jnp.clip(drawn, -bound, bound).astype(kind)


def setup_inputs(seed: int = 0) -> dict:
    key_list = jax.random.split(jax.random.key(seed), 10)
    offsets = jnp.clip(1.0 * jax.random.uniform(key_list[0], (3, NXL, NYL, NZL, SLOTS), jnp.float32) ** steps_of(key_list[0], (3, NXL, NYL, NZL, SLOTS), ((1, 4), (2, 4), (3, 2)), -0.2, 0.2), 0.0, 1.0)
    charges = centred(key_list[1], (NXL, NYL, NZL, SLOTS), 0.1, 0.6, ((0, 4), (1, 4), (2, 2)), jnp.float32)
    counts = plant(jax.random.randint(key_list[2], (NXL, NYL, NZL), 1, SLOTS + 1), jax.random.fold_in(key_list[2], 1), 1, SLOTS).astype(jnp.int32)
    owned_cell = jax.random.permutation(key_list[3], PARENTS).astype(jnp.int32)
    list_sources = plant(jax.random.randint(key_list[4], (PARENTS, LIST), 0, PARENTS), jax.random.fold_in(key_list[4], 1), 0, PARENTS - 1).astype(jnp.int32)
    list_ops = plant(jax.random.randint(key_list[5], (PARENTS, LIST), 0, OPS), jax.random.fold_in(key_list[5], 1), 0, OPS - 1).astype(jnp.int32)
    m2m = centred(key_list[6], (8, COEF, COEF), (8 * COEF) ** -0.5, 0.1875, (), jnp.float32)
    m2l = centred(key_list[7], (COEF, COEF, OPS), (COEF * LIST) ** -0.5, 0.0390625)
    l2l = centred(key_list[8], (8, COEF, COEF), COEF ** -0.5, 0.5, (), jnp.float32)
    return {"offsets": offsets, "charges": charges, "counts": counts, "owned_cell": owned_cell, "list_sources": list_sources, "list_ops": list_ops, "m2m": m2m, "m2l": m2l, "l2l": l2l}


softening = 0.01

def harmonics(relative):
    coord_x, coord_y, coord_z = (relative[0], relative[1], relative[2])
    radius2 = coord_x * coord_x + coord_y * coord_y + coord_z * coord_z
    real_part = {}
    imag_part = {}
    real_part[0, 0] = jnp.ones_like(coord_x)
    imag_part[0, 0] = jnp.zeros_like(coord_x)
    for azimuth in range(1, ORDER + 1):
        factor = 1.0 if azimuth == 1 else math.sqrt((2 * azimuth - 1) / (2 * azimuth))
        prev_re = real_part[azimuth - 1, azimuth - 1]
        prev_im = imag_part[azimuth - 1, azimuth - 1]
        real_part[azimuth, azimuth] = factor * (coord_x * prev_re - coord_y * prev_im)
        imag_part[azimuth, azimuth] = factor * (coord_x * prev_im + coord_y * prev_re)
    for azimuth in range(0, ORDER + 1):
        for degree in range(azimuth + 1, ORDER + 1):
            denom = math.sqrt(degree * degree - azimuth * azimuth)
            first = (2 * degree - 1) / denom
            next_re = first * coord_z * real_part[degree - 1, azimuth]
            next_im = first * coord_z * imag_part[degree - 1, azimuth]
            if degree - 2 >= azimuth:
                second = math.sqrt((degree - 1) ** 2 - azimuth * azimuth) / denom
                next_re = next_re - second * radius2 * real_part[degree - 2, azimuth]
                next_im = next_im - second * radius2 * imag_part[degree - 2, azimuth]
            real_part[degree, azimuth] = next_re
            imag_part[degree, azimuth] = next_im
    pieces = []
    for degree in range(ORDER + 1):
        pieces.append(real_part[degree, 0])
        for azimuth in range(1, degree + 1):
            pieces.append(real_part[degree, azimuth])
            pieces.append(imag_part[degree, azimuth])
    return jnp.stack(pieces, 0)

def pair_sum(target, source, delta, self_pair):
    dist2 = jnp.zeros(target.shape[1:] + (source.shape[-1],), jnp.float32)
    for component in range(3):
        diff = target[component][..., :, None] - source[component][..., None, :] - float(delta[component])
        dist2 = dist2 + diff * diff
    inverse = lax.rsqrt(dist2 + softening)
    if self_pair:
        width = source.shape[-1]
        inverse = inverse * (1.0 - jnp.eye(width, dtype=jnp.float32))
    return lax.optimization_barrier(jnp.sum(inverse * source[3][..., None, :], -1))

def deltas():
    result = []
    for step_x in (-1, 0, 1):
        for step_y in (-1, 0, 1):
            for step_z in (-1, 0, 1):
                result.append((step_x, step_y, step_z))
    return result

def child_stack(pieces, coef):
    stacked = jnp.stack(pieces, 0)
    shape = stacked.shape
    stacked = stacked.reshape((2, 2, 2) + shape[1:])
    stacked = jnp.transpose(stacked, (3, 4, 0, 5, 1, 6, 2))
    return stacked.reshape((coef, shape[2] * 2, shape[3] * 2, shape[4] * 2))

def children(field):
    coef, size_x, size_y, size_z = field.shape
    split = field.reshape(coef, size_x // 2, 2, size_y // 2, 2, size_z // 2, 2)
    result = []
    for octant in range(8):
        result.append(split[:, :, octant // 4, :, octant // 2 % 2, :, octant % 2])
    return result

def reference(offsets, charges, counts, owned_cell, list_sources, list_ops, m2m, m2l, l2l):
    slot_ids = jnp.arange(SLOTS, dtype=jnp.int32)
    live = (slot_ids[None, None, None, :] < counts[..., None]).astype(jnp.float32)
    charge_live = charges * live
    stacked = jnp.concatenate([offsets, charge_live[None]], 0)
    padded = jnp.pad(stacked, ((0, 0), (1, 1), (1, 1), (1, 1), (0, 0)))

    def slab(slab_x):
        target = lax.dynamic_index_in_dim(stacked, slab_x, 1, keepdims=False)
        total = jnp.zeros(target.shape[1:], jnp.float32)
        for delta in deltas():
            plane = lax.dynamic_index_in_dim(padded, slab_x + 1 + delta[0], 1, keepdims=False)
            source = plane[:, 1 + delta[1]:1 + delta[1] + NYL, 1 + delta[2]:1 + delta[2] + NZL]
            total = total + pair_sum(target, source, delta, delta == (0, 0, 0))
        return total
    near = lax.map(slab, jnp.arange(NXL, dtype=jnp.int32))
    basis = harmonics(offsets - 0.5)
    coef = basis.shape[0]
    leaf_multipole = lax.optimization_barrier(jnp.sum(basis * charge_live[None], -1))
    parent = jnp.zeros((coef, NXL // 2, NYL // 2, NZL // 2), jnp.float32)
    for octant, child in enumerate(children(leaf_multipole)):
        parent = parent + jnp.tensordot(m2m[octant], child, axes=(1, 0), precision=lax.Precision.HIGHEST)
    parent_bf = parent.astype(jnp.bfloat16).reshape(coef, PARENTS)
    sources = parent_bf.astype(jnp.float32)[:, list_sources]
    onehot = (list_ops[..., None] == jnp.arange(OPS, dtype=jnp.int32)).astype(jnp.float32)
    grouped = jnp.einsum('rek,cre->rck', onehot, sources, precision=lax.Precision.HIGHEST).astype(jnp.bfloat16)
    owner_local = jnp.einsum('abk,rbk->ra', m2l.astype(jnp.float32), grouped.astype(jnp.float32), precision=lax.Precision.HIGHEST)
    parent_local = jnp.zeros((PARENTS, coef), jnp.float32).at[owned_cell].set(owner_local)
    parent_local = parent_local.T.reshape(coef, NXL // 2, NYL // 2, NZL // 2)
    pieces = [jnp.tensordot(l2l[octant], parent_local, axes=(1, 0), precision=lax.Precision.HIGHEST) for octant in range(8)]
    leaf_local = child_stack(pieces, coef)
    far = lax.optimization_barrier(jnp.sum(basis * leaf_local[..., None], 0))
    return live * (near + far)
```

```python
import math
import functools
import numpy as np
import jax
import jax.numpy as jnp
from jax import lax
from jax.experimental import pallas as pl
from jax.experimental.pallas import tpu as pltpu
from jax.sharding import PartitionSpec as P

SOFTENING = 0.01
DELTAS = [(dx, dy, dz) for dx in (-1, 0, 1) for dy in (-1, 0, 1) for dz in (-1, 0, 1)]


def delta_tables():
    table = np.zeros((27, 64, 128), np.float32)
    for index, delta in enumerate(DELTAS):
        for axis in range(3):
            for group in range(3):
                table[index, 8 * group + axis] = 2.0 * delta[axis]
                table[index, 32 + 8 * group + axis] = delta[axis]
        table[index, 24] = sum(d * d for d in delta)
    return table


def split3(value):
    first = value.astype(jnp.bfloat16).astype(jnp.float32)
    rest = value - first
    second = rest.astype(jnp.bfloat16).astype(jnp.float32)
    third = (rest - second).astype(jnp.bfloat16).astype(jnp.float32)
    return first, second, third


def rows_of(raw, shape):
    rows = lax.broadcasted_iota(jnp.int32, shape, 0)
    padded = jnp.concatenate([raw, jnp.zeros_like(raw)], 0)
    centred = jnp.where(rows < 3, padded - 0.5, 0.0)
    square = centred * centred
    norm = square[0:1] + square[1:2] + square[2:3]
    return rows, centred, norm


def pick(rows, low, parts, high):
    first, second, third = parts
    out = jnp.where(rows == low, first, high)
    out = jnp.where(rows == low + 1, second, out)
    return jnp.where(rows == low + 2, third, out)


def source_features(raw, shape):
    rows, centred, norm = rows_of(raw, shape)
    one, two, three = split3(centred)
    ones = jnp.where((rows >= 3) & (rows < 6), 1.0, 0.0)
    norms = pick(rows, 0, split3(norm), ones)
    zero = jnp.zeros_like(one)
    first_row = jnp.where(rows == 0, 1.0, 0.0)
    groups = [one, one, one, two, two, three, norms, zero, one, two, three, first_row]
    return jnp.concatenate(groups, 0).astype(jnp.bfloat16)


def target_features(raw, shape):
    rows, centred, norm = rows_of(raw, shape)
    one, two, three = split3(centred)
    one, two, three = -2.0 * one, -2.0 * two, -2.0 * three
    lead = jnp.where(rows < 3, 1.0, 0.0)
    norms = pick(rows, 3, split3(norm + SOFTENING), lead)
    zero = jnp.zeros_like(one)
    first_row = jnp.where(rows == 0, 1.0, 0.0)
    groups = [one, two, three, one, two, one, norms, zero]
    groups += [lead, lead, lead, first_row, one, two, three, zero]
    return jnp.concatenate(groups, 0).T.astype(jnp.bfloat16)


def near_body(cells, counts, source, table, out, base, left, total):
    cells_x, cells_y, cells_z = cells
    pad_y, pad_z = cells_y + 2, cells_z + 2
    leaves = cells_x * cells_y * cells_z
    width = source.shape[-1]
    shape = (8, width)
    padded = source.shape[0]

    def fill(leaf, carry):
        base[leaf] = source_features(source[leaf], shape)
        return carry

    lax.fori_loop(0, padded, fill, 0, unroll=4)

    def home(leaf):
        a = leaf // (cells_y * cells_z)
        b = leaf // cells_z % cells_y
        c = leaf % cells_z
        return ((a + 1) * pad_y + b + 1) * pad_z + c + 1

    def fill_left(leaf, carry):
        left[leaf] = target_features(source[home(leaf)], shape)
        return carry

    lax.fori_loop(0, leaves, fill_left, 0, unroll=2)

    def block(leaf, height):
        centre = home(leaf)
        lhs = left[leaf, 0:height]
        acc = jnp.zeros((height, 128), jnp.float32)
        for index, (dx, dy, dz) in enumerate(DELTAS):
            other = centre + (dx * pad_y + dy) * pad_z + dz
            scale = table[index, 0:32]
            fixed = table[index, 32:64]
            halves = []
            for part in range(width // 128):
                lanes = slice(128 * part, 128 * part + 128)
                halves.append(
                    jnp.concatenate(
                        [base[other, 0:64, lanes], base[other, 64:96, lanes] * scale, fixed], 0
                    )
                )
            rhs = jnp.concatenate(halves, 1)
            dist2 = jnp.dot(lhs, rhs, preferred_element_type=jnp.float32)
            inverse = lax.rsqrt(dist2)
            if dx == 0 and dy == 0 and dz == 0:
                row = lax.broadcasted_iota(jnp.int32, inverse.shape, 0)
                col = lax.broadcasted_iota(jnp.int32, inverse.shape, 1)
                inverse = jnp.where(row == col, 0.0, inverse)
            weighted = inverse * source[other, 3:4]
            for part in range(width // 128):
                acc = acc + weighted[:, 128 * part : 128 * part + 128]
        total[leaf, 0:height] = acc

    step = 64

    def leaf_step(leaf, carry):
        pieces = (counts[leaf] + step - 1) // step
        for number in range(1, width // step + 1):
            last = number == width // step
            hit = (pieces >= number) if last else (pieces == number)

            @pl.when(hit)
            def _():
                block(leaf, number * step)

        return carry

    lax.fori_loop(0, leaves, leaf_step, 0)
    ones = jnp.ones((8, 128), jnp.bfloat16)
    dims = (((1,), (1,)), ((), ()))

    def finish(leaf, carry):
        first, second, third = split3(total[leaf])
        result = jnp.zeros((8, width), jnp.float32)
        for piece in (first, second, third):
            result = result + lax.dot_general(
                ones, piece.astype(jnp.bfloat16), dims, preferred_element_type=jnp.float32
            )
        slot = lax.broadcasted_iota(jnp.int32, (1, width), 1)
        out[pl.ds(leaf, 1), :] = jnp.where(slot < counts[leaf], result[0:1], 0.0)
        return carry

    lax.fori_loop(0, leaves, finish, 0, unroll=4)


def near_field(counts, padded, cells):
    leaves = cells[0] * cells[1] * cells[2]
    total, _, width = padded.shape
    table = jnp.asarray(delta_tables(), jnp.bfloat16)
    vmem = pl.BlockSpec(memory_space=pltpu.VMEM)
    return pl.pallas_call(
        functools.partial(near_body, cells),
        out_shape=jax.ShapeDtypeStruct((leaves, width), jnp.float32),
        in_specs=[pl.BlockSpec(memory_space=pltpu.SMEM), vmem, vmem],
        out_specs=vmem,
        scratch_shapes=[
            pltpu.VMEM((total, 96, width), jnp.bfloat16),
            pltpu.VMEM((leaves, width, 128), jnp.bfloat16),
            pltpu.VMEM((leaves, width, 128), jnp.float32),
        ],
        name="near",
    )(counts, padded, table)


def translate_body(shape_info, mine, table, matrix, out, store, weights, sums, sems):
    coef, per_device, lists, ops, wide = shape_info
    rows = table.shape[0]
    span = 128 // per_device
    blocks = -(-coef // span)
    chunk = sums.shape[0] // sems.shape[0]
    copies = [
        pltpu.make_async_copy(
            matrix.at[pl.ds(chunk * index, chunk)],
            store.at[pl.ds(chunk * index, chunk)],
            sems.at[index],
        )
        for index in range(sems.shape[0])
    ]
    for copy in copies:
        copy.start()

    def iota(shape, dim):
        return lax.broadcasted_iota(jnp.int32, shape, dim)

    def mask(condition):
        return jnp.where(condition, 1.0, 0.0)

    seg = 256
    head = table[:, 0:128].astype(jnp.float32)
    owned = head[:, coef : coef + 1] + 256.0 * head[:, coef + 1 : coef + 2]
    lane = iota((rows, 128), 1)
    chosen = mask((owned.astype(jnp.int32) == lane + mine[0]) & (lane < per_device))
    chosen = chosen.T[0:8].astype(jnp.bfloat16)
    entries = jnp.dot(chosen, table[:, 128 : 128 + wide * seg], preferred_element_type=jnp.float32)
    sources = entries[:, seg : 2 * seg]
    if wide == 3:
        sources = sources + 256.0 * entries[:, 2 * seg : 3 * seg]
    sources = sources.astype(jnp.int32)
    classes = entries[:, 0:seg].astype(jnp.int32)
    counted = []
    for row in range(per_device):
        from_cell = mask(iota((rows, seg), 0) == sources[row : row + 1])
        to_class = mask(
            (iota((ops, seg), 0) == classes[row : row + 1]) & (iota((ops, seg), 1) < lists)
        )
        counted.append(
            lax.dot_general(
                to_class.astype(jnp.bfloat16),
                from_cell.astype(jnp.bfloat16),
                (((1,), (1,)), ((), ())),
                preferred_element_type=jnp.float32,
            ).astype(jnp.bfloat16)
        )
    counted = jnp.concatenate(counted, 1)
    parents = table[:, 0:128]
    lane = iota((rows, 128), 1)
    for block in range(blocks):
        pick_row = iota((128, 128), 0)
        pick_col = iota((128, 128), 1)
        spread = mask((pick_row == span * block + pick_col % span) & (pick_row < coef))
        tiled = jnp.dot(parents, spread.astype(jnp.bfloat16), preferred_element_type=jnp.float32)
        stacked = jnp.concatenate(
            [jnp.where(lane // span == row, tiled, 0.0) for row in range(per_device)], 0
        )
        weights[block] = jnp.dot(
            counted, stacked.astype(jnp.bfloat16), preferred_element_type=jnp.float32
        ).astype(jnp.bfloat16)
    for index, copy in enumerate(copies):
        copy.wait()
        total = jnp.zeros((chunk, 128), jnp.float32)
        for block in range(blocks):
            height = min(span, coef - span * block)
            part = store[pl.ds(chunk * index, chunk), span * block : span * block + height, :]
            if height < span:
                fill = jnp.zeros((chunk, span - height, ops), part.dtype)
                part = jnp.concatenate([part, fill], 1)
            result = jnp.dot(
                part.reshape(chunk * span, ops), weights[block], preferred_element_type=jnp.float32
            ).reshape(chunk, span, 128)
            keep = iota((chunk, span, 128), 1) == iota((chunk, span, 128), 2) % span
            total = total + jnp.sum(jnp.where(keep, result, 0.0), 1)
        sums[pl.ds(chunk * index, chunk), :] = total
    gather = mask(iota((128, 128), 0) // span == iota((128, 128), 1)).astype(jnp.bfloat16)
    local = jnp.zeros((coef, 128), jnp.float32)
    for piece in split3(sums[...]):
        local = local + jnp.dot(
            piece.astype(jnp.bfloat16), gather, preferred_element_type=jnp.float32
        )
    out[...] = local


def translate(mine, table, matrix, per_device, lists, wide):
    coef, _, ops = matrix.shape
    pieces = next(n for n in range(11, 0, -1) if coef % n == 0)
    vmem = pl.BlockSpec(memory_space=pltpu.VMEM)
    span = 128 // per_device
    return pl.pallas_call(
        functools.partial(translate_body, (coef, per_device, lists, ops, wide)),
        out_shape=jax.ShapeDtypeStruct((coef, 128), jnp.float32),
        in_specs=[pl.BlockSpec(memory_space=pltpu.SMEM), vmem, pl.BlockSpec(memory_space=pl.ANY)],
        out_specs=vmem,
        scratch_shapes=[
            pltpu.VMEM(matrix.shape, matrix.dtype),
            pltpu.VMEM((-(-coef // span), ops, 128), jnp.bfloat16),
            pltpu.VMEM((coef, 128), jnp.float32),
            pltpu.SemaphoreType.DMA((pieces,)),
        ],
        name="translate",
    )(mine, table, matrix)


ORDER = 10
MESH_AXES = ("gx", "gy", "gz")


def extended(value, sides):
    for axis, dim in sides:
        peers, length = lax.axis_size(axis), value.shape[dim]
        last = lax.slice_in_dim(value, length - 1, length, axis=dim)
        leading = lax.slice_in_dim(value, 0, 1, axis=dim)
        if peers == 2:
            upper = lax.axis_index(axis) == 1
            other = lax.ppermute(jnp.where(upper, leading, last), axis, [(0, 1), (1, 0)])
            before = jnp.where(upper, other, 0.0)
            after = jnp.where(upper, 0.0, other)
        else:
            up = [(i, i + 1) for i in range(peers - 1)]
            before = lax.ppermute(last, axis, up)
            after = lax.ppermute(leading, axis, [(j, i) for i, j in up])
        value = jnp.concatenate([before, value, after], axis=dim)
    return value


def harmonics(relative):
    coord_x, coord_y, coord_z = (relative[0], relative[1], relative[2])
    radius2 = coord_x * coord_x + coord_y * coord_y + coord_z * coord_z
    real_part = {}
    imag_part = {}
    real_part[0, 0] = jnp.ones_like(coord_x)
    imag_part[0, 0] = jnp.zeros_like(coord_x)
    for azimuth in range(1, ORDER + 1):
        factor = 1.0 if azimuth == 1 else math.sqrt((2 * azimuth - 1) / (2 * azimuth))
        prev_re = real_part[azimuth - 1, azimuth - 1]
        prev_im = imag_part[azimuth - 1, azimuth - 1]
        real_part[azimuth, azimuth] = factor * (coord_x * prev_re - coord_y * prev_im)
        imag_part[azimuth, azimuth] = factor * (coord_x * prev_im + coord_y * prev_re)
    for azimuth in range(0, ORDER + 1):
        for degree in range(azimuth + 1, ORDER + 1):
            denom = math.sqrt(degree * degree - azimuth * azimuth)
            first = (2 * degree - 1) / denom
            next_re = first * coord_z * real_part[degree - 1, azimuth]
            next_im = first * coord_z * imag_part[degree - 1, azimuth]
            if degree - 2 >= azimuth:
                second = math.sqrt((degree - 1) ** 2 - azimuth * azimuth) / denom
                next_re = next_re - second * radius2 * real_part[degree - 2, azimuth]
                next_im = next_im - second * radius2 * imag_part[degree - 2, azimuth]
            real_part[degree, azimuth] = next_re
            imag_part[degree, azimuth] = next_im
    pieces = []
    for degree in range(ORDER + 1):
        pieces.append(real_part[degree, 0])
        for azimuth in range(1, degree + 1):
            pieces.append(real_part[degree, azimuth])
            pieces.append(imag_part[degree, azimuth])
    return pieces


def children(field):
    coef, size_x, size_y, size_z = field.shape
    split = field.reshape(coef, size_x // 2, 2, size_y // 2, 2, size_z // 2, 2)
    result = []
    for octant in range(8):
        result.append(split[:, :, octant // 4, :, octant // 2 % 2, :, octant % 2])
    return result


def columns(cell, halves, peers):
    (half_x, half_y, half_z), (_, count_y, count_z) = halves, peers
    parents_y, parents_z = half_y * count_y, half_z * count_z
    cell_a = cell // (parents_y * parents_z)
    cell_b = cell // parents_z % parents_y
    cell_c = cell % parents_z
    device = (cell_a // half_x * count_y + cell_b // half_y) * count_z + cell_c // half_z
    local = (cell_a % half_x * half_y + cell_b % half_y) * half_z + cell_c % half_z
    return device * (half_x * half_y * half_z) + local


def on_device(offsets, charges, counts, owned_cell, list_sources, list_ops, m2m, m2l, l2l):
    cells = cells_x, cells_y, cells_z = charges.shape[:3]
    width = charges.shape[3]
    leaves = cells_x * cells_y * cells_z
    halves = half_x, half_y, half_z = (cells_x // 2, cells_y // 2, cells_z // 2)
    per_device = half_x * half_y * half_z
    peers = tuple(lax.axis_size(axis) for axis in MESH_AXES)
    devices = peers[0] * peers[1] * peers[2]
    total_parents = per_device * devices
    slot_ids = jnp.arange(width, dtype=jnp.int32)
    live = (slot_ids[None, None, None, :] < counts[..., None]).astype(jnp.float32)
    charge_live = charges * live
    stacked = jnp.stack([offsets[0], offsets[1], offsets[2], charge_live], 3)
    padded = extended(stacked, (("gz", 2), ("gy", 1), ("gx", 0)))
    padded = padded.reshape(-1, 4, width)

    basis = jnp.stack(harmonics(offsets - 0.5), 0)
    coef = basis.shape[0]
    leaf_multipole = jnp.sum(basis * charge_live[None], -1)
    parent = jnp.zeros((coef, half_x, half_y, half_z), jnp.float32)
    for octant, child in enumerate(children(leaf_multipole)):
        parent = parent + jnp.tensordot(
            m2m[octant], child, axes=(1, 0), precision=lax.Precision.HIGHEST
        )
    parent_rows = parent.astype(jnp.bfloat16).reshape(coef, per_device).T

    lists = list_sources.shape[1]
    wide = 2 if total_parents <= 256 else 3
    owner_columns = columns(owned_cell, halves, peers)[:, None]
    source_columns = columns(list_sources, halves, peers)

    def segment(values, size):
        values = values.astype(jnp.bfloat16)
        return jnp.pad(values, ((0, 0), (0, size - values.shape[1])))

    pieces = [
        parent_rows,
        segment(owner_columns % 256, 1),
        segment(owner_columns // 256, 127 - coef),
        segment(list_ops, 256),
        segment(source_columns % 256, 256),
    ]
    if wide == 3:
        pieces.append(segment(source_columns // 256, 256))
    payload = jnp.concatenate(pieces, 1)
    spread = jnp.broadcast_to(payload[None], (devices,) + payload.shape)
    table = lax.all_to_all(spread, MESH_AXES, 0, 0).reshape(total_parents, payload.shape[1])

    near = near_field(counts.reshape(-1), padded, cells).reshape(charges.shape)

    mine = (lax.axis_index(MESH_AXES) * per_device).astype(jnp.int32).reshape(1)
    local = translate(mine, table, m2l, per_device, lists, wide)
    parent_local = local[:, :per_device].reshape(coef, half_x, half_y, half_z)
    pieces = [
        jnp.tensordot(l2l[octant], parent_local, axes=(1, 0), precision=lax.Precision.HIGHEST)
        for octant in range(8)
    ]
    joined = jnp.stack(pieces, 0).reshape((2, 2, 2, coef, half_x, half_y, half_z))
    leaf_local = jnp.transpose(joined, (3, 4, 0, 5, 1, 6, 2)).reshape(
        coef, cells_x, cells_y, cells_z
    )
    far = jnp.sum(basis * leaf_local[..., None], 0)
    return live * (near + far)


def solution(mesh):
    placed = (
        P(None, "gx", "gy", "gz", None),
        P("gx", "gy", "gz", None),
        P("gx", "gy", "gz"),
        P(("gx", "gy", "gz")),
        P(("gx", "gy", "gz"), None),
        P(("gx", "gy", "gz"), None),
        P(),
        P(),
        P(),
    )
    return jax.shard_map(
        on_device, mesh=mesh, in_specs=placed, out_specs=P("gx", "gy", "gz", None), check_vma=False
    )
```

```python
import math
import functools
import numpy as np
import jax
import jax.numpy as jnp
from jax import lax
from jax.experimental import pallas as pl
from jax.experimental.pallas import tpu as pltpu
from jax.sharding import PartitionSpec as P

ORDER = 10
SOFTENING = 0.01
DELTAS = [(dx, dy, dz) for dx in (-1, 0, 1) for dy in (-1, 0, 1) for dz in (-1, 0, 1)]


def delta_tables():
    table = np.zeros((27, 64, 128), np.float32)
    for index, delta in enumerate(DELTAS):
        for axis in range(3):
            for group in range(3):
                table[index, 8 * group + axis] = 2.0 * delta[axis]
                table[index, 32 + 8 * group + axis] = delta[axis]
        table[index, 24] = sum(d * d for d in delta)
    return table


def split3(value):
    first = value.astype(jnp.bfloat16).astype(jnp.float32)
    rest = value - first
    second = rest.astype(jnp.bfloat16).astype(jnp.float32)
    third = (rest - second).astype(jnp.bfloat16).astype(jnp.float32)
    return first, second, third


def rows_of(raw, shape):
    rows = lax.broadcasted_iota(jnp.int32, shape, 0)
    padded = jnp.concatenate([raw, jnp.zeros_like(raw)], 0)
    centred = jnp.where(rows < 3, padded - 0.5, 0.0)
    square = centred * centred
    norm = square[0:1] + square[1:2] + square[2:3]
    return rows, centred, norm


def pick(rows, low, parts, high):
    first, second, third = parts
    out = jnp.where(rows == low, first, high)
    out = jnp.where(rows == low + 1, second, out)
    return jnp.where(rows == low + 2, third, out)


def source_features(raw, shape):
    rows, centred, norm = rows_of(raw, shape)
    one, two, three = split3(centred)
    ones = jnp.where((rows >= 3) & (rows < 6), 1.0, 0.0)
    norms = pick(rows, 0, split3(norm), ones)
    zero = jnp.zeros_like(one)
    first_row = jnp.where(rows == 0, 1.0, 0.0)
    groups = [one, one, one, two, two, three, norms, zero, one, two, three, first_row]
    return jnp.concatenate(groups, 0).astype(jnp.bfloat16)


def target_features(raw, shape):
    rows, centred, norm = rows_of(raw, shape)
    one, two, three = split3(centred)
    one, two, three = -2.0 * one, -2.0 * two, -2.0 * three
    lead = jnp.where(rows < 3, 1.0, 0.0)
    norms = pick(rows, 3, split3(norm + SOFTENING), lead)
    zero = jnp.zeros_like(one)
    first_row = jnp.where(rows == 0, 1.0, 0.0)
    groups = [one, two, three, one, two, one, norms, zero]
    groups += [lead, lead, lead, first_row, one, two, three, zero]
    return jnp.concatenate(groups, 0).T.astype(jnp.bfloat16)


def near_body(cells, counts, source, table, out, base, left, total):
    cells_x, cells_y, cells_z = cells
    pad_y, pad_z = cells_y + 2, cells_z + 2
    leaves = cells_x * cells_y * cells_z
    width = source.shape[-1]
    shape = (8, width)
    padded = source.shape[0]

    def fill(leaf, carry):
        base[leaf] = source_features(source[leaf], shape)
        return carry

    lax.fori_loop(0, padded, fill, 0, unroll=4)

    def home(leaf):
        a = leaf // (cells_y * cells_z)
        b = leaf // cells_z % cells_y
        c = leaf % cells_z
        return ((a + 1) * pad_y + b + 1) * pad_z + c + 1

    def fill_left(leaf, carry):
        left[leaf] = target_features(source[home(leaf)], shape)
        return carry

    lax.fori_loop(0, leaves, fill_left, 0, unroll=2)

    def block(leaf, height):
        centre = home(leaf)
        lhs = left[leaf, 0:height]
        acc = jnp.zeros((height, 128), jnp.float32)
        for index, (dx, dy, dz) in enumerate(DELTAS):
            other = centre + (dx * pad_y + dy) * pad_z + dz
            scale = table[index, 0:32]
            fixed = table[index, 32:64]
            halves = []
            for part in range(width // 128):
                lanes = slice(128 * part, 128 * part + 128)
                halves.append(
                    jnp.concatenate(
                        [base[other, 0:64, lanes], base[other, 64:96, lanes] * scale, fixed], 0
                    )
                )
            rhs = jnp.concatenate(halves, 1)
            dist2 = jnp.dot(lhs, rhs, preferred_element_type=jnp.float32)
            inverse = lax.rsqrt(dist2)
            if dx == 0 and dy == 0 and dz == 0:
                row = lax.broadcasted_iota(jnp.int32, inverse.shape, 0)
                col = lax.broadcasted_iota(jnp.int32, inverse.shape, 1)
                inverse = jnp.where(row == col, 0.0, inverse)
            weighted = inverse * source[other, 3:4]
            for part in range(width // 128):
                acc = acc + weighted[:, 128 * part : 128 * part + 128]
        total[leaf, 0:height] = acc

    step = 64

    def leaf_step(leaf, carry):
        pieces = (counts[leaf] + step - 1) // step
        for number in range(1, width // step + 1):
            last = number == width // step
            hit = (pieces >= number) if last else (pieces == number)

            @pl.when(hit)
            def _():
                block(leaf, number * step)

        return carry

    lax.fori_loop(0, leaves, leaf_step, 0)
    ones = jnp.ones((8, 128), jnp.bfloat16)
    dims = (((1,), (1,)), ((), ()))

    def finish(leaf, carry):
        first, second, third = split3(total[leaf])
        result = jnp.zeros((8, width), jnp.float32)
        for piece in (first, second, third):
            result = result + lax.dot_general(
                ones, piece.astype(jnp.bfloat16), dims, preferred_element_type=jnp.float32
            )
        slot = lax.broadcasted_iota(jnp.int32, (1, width), 1)
        out[pl.ds(leaf, 1), :] = jnp.where(slot < counts[leaf], result[0:1], 0.0)
        return carry

    lax.fori_loop(0, leaves, finish, 0, unroll=4)


def near_field(counts, padded, cells):
    leaves = cells[0] * cells[1] * cells[2]
    total, _, width = padded.shape
    table = jnp.asarray(delta_tables(), jnp.bfloat16)
    vmem = pl.BlockSpec(memory_space=pltpu.VMEM)
    return pl.pallas_call(
        functools.partial(near_body, cells),
        out_shape=jax.ShapeDtypeStruct((leaves, width), jnp.float32),
        in_specs=[pl.BlockSpec(memory_space=pltpu.SMEM), vmem, vmem],
        out_specs=vmem,
        scratch_shapes=[
            pltpu.VMEM((total, 96, width), jnp.bfloat16),
            pltpu.VMEM((leaves, width, 128), jnp.bfloat16),
            pltpu.VMEM((leaves, width, 128), jnp.float32),
        ],
        name="near",
    )(counts, padded, table)


def emit_harmonics(coord_x, coord_y, coord_z, emit):
    radius2 = coord_x * coord_x + coord_y * coord_y + coord_z * coord_z

    def give(degree, azimuth, real, imag):
        if azimuth == 0:
            emit(degree * degree, real)
        else:
            emit(degree * degree + 2 * azimuth - 1, real)
            emit(degree * degree + 2 * azimuth, imag)

    top_re, top_im = jnp.ones_like(coord_x), None
    for azimuth in range(ORDER + 1):
        if azimuth == 1:
            top_re, top_im = coord_x, coord_y
        elif azimuth > 1:
            factor = math.sqrt((2 * azimuth - 1) / (2 * azimuth))
            top_re, top_im = (
                factor * (coord_x * top_re - coord_y * top_im),
                factor * (coord_x * top_im + coord_y * top_re),
            )
        give(azimuth, azimuth, top_re, top_im)
        older, newer = None, (top_re, top_im)
        for degree in range(azimuth + 1, ORDER + 1):
            denom = math.sqrt(degree * degree - azimuth * azimuth)
            scaled = ((2 * degree - 1) / denom) * coord_z
            lower = None
            if degree - 2 >= azimuth:
                lower = (math.sqrt((degree - 1) ** 2 - azimuth * azimuth) / denom) * radius2
            values = []
            for part in range(1 if azimuth == 0 else 2):
                value = scaled * newer[part]
                if lower is not None:
                    value = value - lower * older[part]
                values.append(value)
            older, newer = newer, tuple(values)
            give(degree, azimuth, values[0], values[-1])


def fill_basis(coords, basis):
    leaves = coords.shape[1]
    for first in range(0, leaves, 8):
        rows = slice(first, first + 8)
        x, y, z = (coords[axis, rows, :] - 0.5 for axis in range(3))

        def emit(index, value):
            basis[index, rows, :] = value

        emit_harmonics(x, y, z, emit)


def child_leaf(parent, octant, cells):
    _, cells_y, cells_z = cells
    half_y, half_z = cells_y // 2, cells_z // 2
    a = parent // (half_y * half_z)
    b = parent // half_z % half_y
    c = parent % half_z
    x = 2 * a + octant // 4
    y = 2 * b + octant // 2 % 2
    z = 2 * c + octant % 2
    return (x * cells_y + y) * cells_z + z


def iota(shape, dim):
    return lax.broadcasted_iota(jnp.int32, shape, dim)


def mask(condition):
    return jnp.where(condition, 1.0, 0.0)


def narrow(value):
    return value.astype(jnp.bfloat16)


def multiply(left, right, dims=(((1,), (0,)), ((), ()))):
    return lax.dot_general(narrow(left), narrow(right), dims, preferred_element_type=jnp.float32)


def multipole_body(cells, coords, charge, upward, out, basis, sums):
    leaves, width = charge.shape
    coef = upward.shape[1]
    per_device = leaves // 8
    fill_basis(coords, basis)
    parts = jnp.concatenate(split3(charge[...]) + (jnp.zeros((128 - 3 * leaves, width)),), 0)
    columns_all = parts.T
    lane = iota((width, 128), 1)
    chunk = next(n for n in range(11, 0, -1) if coef % n == 0)
    rights = [narrow(jnp.where(lane < leaves * (3 - j), columns_all, 0.0)) for j in range(3)]
    keep = iota((chunk, leaves, 128), 1) == iota((chunk, leaves, 128), 2) % leaves
    for start in range(0, coef, chunk):
        lefts = split3(basis[start : start + chunk].reshape(chunk * leaves, width))
        result = sum(multiply(left, right) for left, right in zip(lefts, rights))
        result = jnp.where(keep, result.reshape(chunk, leaves, 128), 0.0)
        sums[start : start + chunk, :] = jnp.sum(result, 1)
    folded = sums[...]
    folded = folded + pltpu.roll(folded, 128 - leaves, 1) + pltpu.roll(folded, 128 - 2 * leaves, 1)
    lane = iota((coef, 128), 1)
    first, second, third = split3(folded)
    stacked = jnp.where(lane < leaves, first, 0.0)
    stacked = jnp.where(lane // leaves == 1, pltpu.roll(second, leaves, 1), stacked)
    stacked = jnp.where(lane // leaves == 2, pltpu.roll(third, 2 * leaves, 1), stacked)
    span = 128 // per_device
    row, col = iota((128, 128), 0), iota((128, 128), 1)
    slot = col % span
    wanted = child_leaf(col // span, slot // 3, cells) + leaves * (slot % 3)
    chosen = multiply(stacked, mask((row == wanted) & (slot < 24)))
    slot = lane % span
    result = jnp.zeros((coef, 128), jnp.float32)
    for octant in range(8):
        for j, left in enumerate(split3(upward[octant])):
            right = jnp.where((slot >= 3 * octant) & (slot < 3 * octant + 3 - j), chosen, 0.0)
            result = result + multiply(left, right)
    out[...] = narrow(jnp.sum(result.T.reshape(per_device, span, coef), 1))


def multipole(coords, charge, upward, cells):
    leaves, width = charge.shape
    coef = upward.shape[1]
    vmem = pl.BlockSpec(memory_space=pltpu.VMEM)
    return pl.pallas_call(
        functools.partial(multipole_body, cells),
        out_shape=jax.ShapeDtypeStruct((leaves // 8, coef), jnp.bfloat16),
        in_specs=[vmem] * 3,
        out_specs=vmem,
        scratch_shapes=[
            pltpu.VMEM((coef, leaves, width), jnp.float32),
            pltpu.VMEM((coef, 128), jnp.float32),
        ],
        name="multipole",
    )(coords, charge, upward)


def translate_body(info, mine, counts, table, matrix, coords, near, downward, out, *scratch):
    cells, per_device, lists, wide = info
    weights, sums, basis, spread_local = scratch
    coef, _, ops = matrix.shape
    leaves, width = coords.shape[1:]
    rows = table.shape[0]
    span = 128 // per_device
    blocks = -(-coef // span)
    chunk = next(n for n in range(11, 0, -1) if coef % n == 0)
    fill_basis(coords, basis)

    seg = 256
    head = table[:, 0:128].astype(jnp.float32)
    owned = head[:, coef : coef + 1] + 256.0 * head[:, coef + 1 : coef + 2]
    lane = iota((rows, 128), 1)
    chosen = mask((owned.astype(jnp.int32) == lane + mine[0]) & (lane < per_device))
    entries = multiply(chosen.T[0:8], table[:, 128 : 128 + wide * seg])
    sources = entries[:, seg : 2 * seg]
    if wide == 3:
        sources = sources + 256.0 * entries[:, 2 * seg : 3 * seg]
    sources = sources.astype(jnp.int32)
    classes = entries[:, 0:seg].astype(jnp.int32)
    across = (((1,), (1,)), ((), ()))
    counted = []
    for row in range(per_device):
        from_cell = mask(iota((rows, seg), 0) == sources[row : row + 1])
        to_class = iota((ops, seg), 0) == classes[row : row + 1]
        to_class = mask(to_class & (iota((ops, seg), 1) < lists))
        counted.append(narrow(multiply(to_class, from_cell, across)))
    counted = jnp.concatenate(counted, 1)
    parents = table[:, 0:128]
    for block in range(blocks):
        row, col = iota((128, 128), 0), iota((128, 128), 1)
        tiled = multiply(parents, mask((row == span * block + col % span) & (row < coef)))
        stacked = [jnp.where(lane // span == row, tiled, 0.0) for row in range(per_device)]
        weights[block] = narrow(multiply(counted, jnp.concatenate(stacked, 0)))
    for start in range(0, coef, chunk):
        total = jnp.zeros((chunk, 128), jnp.float32)
        for block in range(blocks):
            height = min(span, coef - span * block)
            part = matrix[start : start + chunk, span * block : span * block + height, :]
            if height < span:
                fill = jnp.zeros((chunk, span - height, ops), part.dtype)
                part = jnp.concatenate([part, fill], 1)
            result = multiply(part.reshape(chunk * span, ops), weights[block])
            result = result.reshape(chunk, span, 128)
            keep = iota((chunk, span, 128), 1) == iota((chunk, span, 128), 2) % span
            total = total + jnp.sum(jnp.where(keep, result, 0.0), 1)
        sums[start : start + chunk, :] = total
    gather = mask(iota((128, 128), 0) // span == iota((128, 128), 1))
    local = sum(multiply(piece, gather) for piece in split3(sums[...]))
    local = jnp.concatenate(split3(local.T[0:8]), 0)
    for octant in range(8):
        result = jnp.zeros((8, coef), jnp.float32)
        for j, right in enumerate(split3(downward[octant])):
            product = multiply(local, right, across)
            for i in range(3 - j):
                result = result + product[8 * i : 8 * i + 8]
        for parent in range(per_device):
            leaf = child_leaf(parent, octant, cells)
            spread_local[leaf : leaf + 1, 0:coef] = result[parent : parent + 1]
    slot = iota((8, width), 1)
    sub = iota((8, width), 0)
    for first in range(0, leaves, 8):
        values = spread_local[first : first + 8, :]
        total = near[first : first + 8, :]
        for index in range(coef):
            column = jnp.broadcast_to(values[:, index : index + 1], (8, width))
            total = total + column * basis[index, first : first + 8, :]
        limit = jnp.zeros((8, width), jnp.int32)
        for row in range(8):
            limit = jnp.where(sub == row, counts[first + row], limit)
        out[first : first + 8, :] = jnp.where(slot < limit, total, 0.0)


def translate(mine, counts, table, matrix, coords, near, downward, cells, lists, wide):
    coef, _, ops = matrix.shape
    leaves, width = near.shape
    per_device = leaves // 8
    span = 128 // per_device
    smem = pl.BlockSpec(memory_space=pltpu.SMEM)
    vmem = pl.BlockSpec(memory_space=pltpu.VMEM)
    return pl.pallas_call(
        functools.partial(translate_body, (cells, per_device, lists, wide)),
        out_shape=jax.ShapeDtypeStruct((leaves, width), jnp.float32),
        in_specs=[smem, smem] + [vmem] * 5,
        out_specs=vmem,
        scratch_shapes=[
            pltpu.VMEM((-(-coef // span), ops, 128), jnp.bfloat16),
            pltpu.VMEM((coef, 128), jnp.float32),
            pltpu.VMEM((coef, leaves, width), jnp.float32),
            pltpu.VMEM((leaves, 128), jnp.float32),
        ],
        name="translate",
    )(mine, counts, table, matrix, coords, near, downward)


MESH_AXES = ("gx", "gy", "gz")


def extended(value, sides):
    for axis, dim in sides:
        peers, length = lax.axis_size(axis), value.shape[dim]
        last = lax.slice_in_dim(value, length - 1, length, axis=dim)
        leading = lax.slice_in_dim(value, 0, 1, axis=dim)
        if peers == 2:
            upper = lax.axis_index(axis) == 1
            other = lax.ppermute(jnp.where(upper, leading, last), axis, [(0, 1), (1, 0)])
            before = jnp.where(upper, other, 0.0)
            after = jnp.where(upper, 0.0, other)
        else:
            up = [(i, i + 1) for i in range(peers - 1)]
            before = lax.ppermute(last, axis, up)
            after = lax.ppermute(leading, axis, [(j, i) for i, j in up])
        value = jnp.concatenate([before, value, after], axis=dim)
    return value


def columns(cell, halves, peers):
    (half_x, half_y, half_z), (_, count_y, count_z) = halves, peers
    parents_y, parents_z = half_y * count_y, half_z * count_z
    cell_a = cell // (parents_y * parents_z)
    cell_b = cell // parents_z % parents_y
    cell_c = cell % parents_z
    device = (cell_a // half_x * count_y + cell_b // half_y) * count_z + cell_c // half_z
    local = (cell_a % half_x * half_y + cell_b % half_y) * half_z + cell_c % half_z
    return device * (half_x * half_y * half_z) + local


def on_device(offsets, charges, counts, owned_cell, list_sources, list_ops, m2m, m2l, l2l):
    cells = cells_x, cells_y, cells_z = charges.shape[:3]
    width = charges.shape[3]
    leaves = cells_x * cells_y * cells_z
    halves = half_x, half_y, half_z = (cells_x // 2, cells_y // 2, cells_z // 2)
    per_device = half_x * half_y * half_z
    peers = tuple(lax.axis_size(axis) for axis in MESH_AXES)
    devices = peers[0] * peers[1] * peers[2]
    total_parents = per_device * devices
    slot_ids = jnp.arange(width, dtype=jnp.int32)
    live = (slot_ids[None, None, None, :] < counts[..., None]).astype(jnp.float32)
    charge_live = charges * live
    stacked = jnp.stack([offsets[0], offsets[1], offsets[2], charge_live], 3)
    padded = extended(stacked, (("gz", 2), ("gy", 1), ("gx", 0)))
    padded = padded.reshape(-1, 4, width)

    coef = m2m.shape[1]
    coords = offsets.reshape(3, leaves, width)
    parent_rows = multipole(coords, charge_live.reshape(leaves, width), m2m, cells)

    lists = list_sources.shape[1]
    wide = 2 if total_parents <= 256 else 3
    owner_columns = columns(owned_cell, halves, peers)[:, None]
    source_columns = columns(list_sources, halves, peers)

    def segment(values, size):
        values = values.astype(jnp.bfloat16)
        return jnp.pad(values, ((0, 0), (0, size - values.shape[1])))

    pieces = [
        parent_rows,
        segment(owner_columns % 256, 1),
        segment(owner_columns // 256, 127 - coef),
        segment(list_ops, 256),
        segment(source_columns % 256, 256),
    ]
    if wide == 3:
        pieces.append(segment(source_columns // 256, 256))
    payload = jnp.concatenate(pieces, 1)
    spread = jnp.broadcast_to(payload[None], (devices,) + payload.shape)
    table = lax.all_to_all(spread, MESH_AXES, 0, 0).reshape(total_parents, payload.shape[1])

    flat_counts = counts.reshape(-1)
    near = near_field(flat_counts, padded, cells)
    mine = (lax.axis_index(MESH_AXES) * per_device).astype(jnp.int32).reshape(1)
    result = translate(mine, flat_counts, table, m2l, coords, near, l2l, cells, lists, wide)
    return result.reshape(charges.shape)


def solution(mesh):
    placed = (
        P(None, "gx", "gy", "gz", None),
        P("gx", "gy", "gz", None),
        P("gx", "gy", "gz"),
        P(("gx", "gy", "gz")),
        P(("gx", "gy", "gz"), None),
        P(("gx", "gy", "gz"), None),
        P(),
        P(),
        P(),
    )
    return jax.shard_map(
        on_device, mesh=mesh, in_specs=placed, out_specs=P("gx", "gy", "gz", None), check_vma=False
    )
```

```python
import math
import functools
import numpy as np
import jax
import jax.numpy as jnp
from jax import lax
from jax.experimental import pallas as pl
from jax.experimental.pallas import tpu as pltpu
from jax.sharding import PartitionSpec as P


ORDER = 10
SOFTENING = 0.01
DELTAS = [(dx, dy, dz) for dx in (-1, 0, 1) for dy in (-1, 0, 1) for dz in (-1, 0, 1)]
DEPTH = 80


def delta_tables():
    table = np.zeros((27, 32, 128), np.float32)
    for index, delta in enumerate(DELTAS):
        for axis in range(3):
            for group in range(3):
                table[index, 3 * group + axis] = 2.0 * delta[axis]
                table[index, 16 + 3 * group + axis] = delta[axis]
        rest = np.float32(sum(d * d for d in delta) + SOFTENING)
        for part in range(3):
            piece = np.asarray(rest).astype(jnp.bfloat16).astype(np.float32)
            table[index, 25 + part] = piece
            rest = np.float32(rest - piece)
    return table


def expand_table():
    table = np.zeros((16, 128), np.float32)
    for axis in range(3):
        first, second, third = axis, 3 + axis, 6 + axis
        for group in range(3):
            table[first, 3 * group + axis] = -2.0
            table[12, 48 + 3 * group + axis] = 1.0
        for group in range(2):
            table[second, 16 + 3 * group + axis] = -2.0
        table[third, 32 + axis] = -2.0
        table[12, 9 + axis] = 1.0
        table[9 + axis, 12 + axis] = 1.0
        for group, source in enumerate((first, second, third)):
            table[source, 64 + 3 * group + axis] = -2.0
        table[12, 73 + axis] = 1.0
    return table


def split3(value):
    first = value.astype(jnp.bfloat16).astype(jnp.float32)
    rest = value - first
    second = rest.astype(jnp.bfloat16).astype(jnp.float32)
    third = (rest - second).astype(jnp.bfloat16).astype(jnp.float32)
    return first, second, third


def iota(shape, dim):
    return lax.broadcasted_iota(jnp.int32, shape, dim)


def mask(condition):
    return jnp.where(condition, 1.0, 0.0)


def narrow(value):
    return value.astype(jnp.bfloat16)


def multiply(left, right, dims=(((1,), (0,)), ((), ()))):
    return lax.dot_general(narrow(left), narrow(right), dims, preferred_element_type=jnp.float32)


def near_body(cells, counts, source, table, expand, out, rows32, base, left, total):
    cells_x, cells_y, cells_z = cells
    _, pad_x, pad_y, pad_z, width = source.shape
    leaves = cells_x * cells_y * cells_z
    tiles = width // 128
    sources = pad_x * pad_y * pad_z

    def fill(column, carry):
        a, b = column // pad_y, column % pad_y
        parts, norm = [], 0.0
        for axis in range(3):
            centred = source[axis, a, b] - 0.5
            norm = norm + centred * centred
            parts.append(split3(centred))
        rows = [parts[axis][part] for part in range(3) for axis in range(3)]
        rows += list(split3(norm)) + [jnp.ones_like(norm)] * 3 + [source[3, a, b]]
        for index, row in enumerate(rows):
            for part in range(tiles):
                start = part * sources * 16 + column * pad_z * 16 + index
                rows32[pl.ds(start, pad_z, stride=16), :] = row[:, 128 * part : 128 * part + 128]
        return carry

    def pack(leaf, carry):
        for part in range(tiles):
            start = pl.multiple_of((part * sources + leaf) * 16, 16)
            base[leaf, :, 128 * part : 128 * part + 128] = narrow(rows32[pl.ds(start, 16), :])
        return carry

    lax.fori_loop(0, pad_x * pad_y, fill, 0)
    lax.fori_loop(0, pad_x * pad_y * pad_z, pack, 0, unroll=8)

    def place(leaf):
        return leaf // (cells_y * cells_z), leaf // cells_z % cells_y, leaf % cells_z

    def home(leaf):
        a, b, c = place(leaf)
        return ((a + 1) * pad_y + b + 1) * pad_z + c + 1

    def count_of(leaf):
        a, b, c = place(leaf)
        return counts[a, b, c]

    def fill_left(leaf):
        features = base[home(leaf)].astype(jnp.float32).T
        left[leaf % 2] = narrow(multiply(features, expand[...]))

    ones = jnp.ones((8, 128), jnp.bfloat16)
    across = (((1,), (1,)), ((), ()))

    def finish(leaf):
        result = sum(multiply(ones, piece, across) for piece in split3(total[leaf % 2]))
        slot = iota((1, width), 1)
        out[pl.ds(leaf, 1), :] = jnp.where(slot < count_of(leaf), result[0:1], 0.0)

    def block(leaf, height):
        centre = home(leaf)
        lhs = left[leaf % 2, 0:height, 0:DEPTH]
        acc = jnp.zeros((height, 128), jnp.float32)
        for index, (dx, dy, dz) in enumerate(DELTAS):
            other = centre + (dx * pad_y + dy) * pad_z + dz
            scale = table[index, 0:16]
            fixed = table[index, 16:32]
            halves = []
            for part in range(tiles):
                feature = base[other, :, 128 * part : 128 * part + 128]
                halves.append(
                    jnp.concatenate([feature, feature, feature, feature * scale, fixed], 0)
                )
            rhs = jnp.concatenate(halves, 1)
            dist2 = jnp.dot(lhs, rhs, preferred_element_type=jnp.float32)
            inverse = lax.rsqrt(dist2)
            if dx == 0 and dy == 0 and dz == 0:
                inverse = jnp.where(iota(inverse.shape, 0) == iota(inverse.shape, 1), 0.0, inverse)
            for part in range(tiles):
                amount = rows32[pl.ds((part * sources + other) * 16 + 15, 1), :]
                acc = acc + inverse[:, 128 * part : 128 * part + 128] * amount
        fill_left(jnp.minimum(leaf + 1, leaves - 1))
        finish(jnp.maximum(leaf - 1, 0))
        total[leaf % 2, 0:height] = acc

    fill_left(0)
    total[...] = jnp.zeros_like(total)
    step = 32

    def choose(leaf, pieces, low, high):
        if high - low == 1:
            block(leaf, high * step)
            return
        middle = (low + high) // 2
        pl.when(pieces <= middle)(lambda: choose(leaf, pieces, low, middle))
        pl.when(pieces > middle)(lambda: choose(leaf, pieces, middle, high))

    def leaf_step(leaf, carry):
        pieces = (count_of(leaf) + step - 1) // step
        choose(leaf, pieces, 0, width // step)
        return carry

    lax.fori_loop(0, leaves, leaf_step, 0)
    finish(leaves - 1)


def near_field(counts, padded, cells):
    leaves = cells[0] * cells[1] * cells[2]
    width = padded.shape[-1]
    sources = padded.shape[1] * padded.shape[2] * padded.shape[3]
    table = jnp.asarray(delta_tables(), jnp.bfloat16)
    expand = jnp.asarray(expand_table(), jnp.bfloat16)
    vmem = pl.BlockSpec(memory_space=pltpu.VMEM)
    return pl.pallas_call(
        functools.partial(near_body, cells),
        out_shape=jax.ShapeDtypeStruct((leaves, width), jnp.float32),
        in_specs=[pl.BlockSpec(memory_space=pltpu.SMEM)] + [vmem] * 3,
        out_specs=vmem,
        scratch_shapes=[
            pltpu.VMEM((sources * 16 * (width // 128), 128), jnp.float32),
            pltpu.VMEM((sources, 16, width), jnp.bfloat16),
            pltpu.VMEM((2, width, 128), jnp.bfloat16),
            pltpu.VMEM((2, width, 128), jnp.float32),
        ],
        name="near",
    )(counts, padded, table, expand)


def emit_harmonics(coord_x, coord_y, coord_z, emit):
    radius2 = coord_x * coord_x + coord_y * coord_y + coord_z * coord_z

    def give(degree, azimuth, real, imag):
        if azimuth == 0:
            emit(degree * degree, real)
        else:
            emit(degree * degree + 2 * azimuth - 1, real)
            emit(degree * degree + 2 * azimuth, imag)

    top_re, top_im = jnp.ones_like(coord_x), None
    for azimuth in range(ORDER + 1):
        if azimuth == 1:
            top_re, top_im = coord_x, coord_y
        elif azimuth > 1:
            factor = math.sqrt((2 * azimuth - 1) / (2 * azimuth))
            top_re, top_im = (
                factor * (coord_x * top_re - coord_y * top_im),
                factor * (coord_x * top_im + coord_y * top_re),
            )
        give(azimuth, azimuth, top_re, top_im)
        older, newer = None, (top_re, top_im)
        for degree in range(azimuth + 1, ORDER + 1):
            denom = math.sqrt(degree * degree - azimuth * azimuth)
            scaled = ((2 * degree - 1) / denom) * coord_z
            lower = None
            if degree - 2 >= azimuth:
                lower = (math.sqrt((degree - 1) ** 2 - azimuth * azimuth) / denom) * radius2
            values = []
            for part in range(1 if azimuth == 0 else 2):
                value = scaled * newer[part]
                if lower is not None:
                    value = value - lower * older[part]
                values.append(value)
            older, newer = newer, tuple(values)
            give(degree, azimuth, values[0], values[-1])


def flatten(field, flat):
    size_x, size_y, size_z = field.shape[:3]
    for a in range(size_x):
        for b in range(size_y):
            first = (a * size_y + b) * size_z
            flat[first : first + size_z, :] = field[a, b]


def fill_basis(offsets, flat, basis):
    leaves = flat.shape[1]
    for axis in range(3):
        flatten(offsets.at[axis], flat.at[axis])
    for first in range(0, leaves, 8):
        rows = slice(first, first + 8)
        x, y, z = (flat[axis, rows, :] - 0.5 for axis in range(3))

        def emit(index, value):
            basis[index, rows, :] = value

        emit_harmonics(x, y, z, emit)


def child_leaf(parent, octant, cells):
    _, cells_y, cells_z = cells
    half_y, half_z = cells_y // 2, cells_z // 2
    a = parent // (half_y * half_z)
    b = parent // half_z % half_y
    c = parent % half_z
    x = 2 * a + octant // 4
    y = 2 * b + octant // 2 % 2
    z = 2 * c + octant % 2
    return (x * cells_y + y) * cells_z + z


def multipole_body(cells, offsets, charges, upward, out, flat, charge, basis, sums):
    leaves, width = charge.shape
    coef = upward.shape[0]
    per_device = leaves // 8
    flatten(charges, charge)
    fill_basis(offsets, flat, basis)
    parts = jnp.concatenate(split3(charge[...]) + (jnp.zeros((128 - 3 * leaves, width)),), 0)
    columns_all = parts.T
    lane = iota((width, 128), 1)
    chunk = next(n for n in range(11, 0, -1) if coef % n == 0)
    rights = [narrow(jnp.where(lane < leaves * (3 - j), columns_all, 0.0)) for j in range(3)]
    keep = iota((chunk, leaves, 128), 1) == iota((chunk, leaves, 128), 2) % leaves
    for start in range(0, coef, chunk):
        lefts = split3(basis[start : start + chunk].reshape(chunk * leaves, width))
        result = sum(multiply(left, right) for left, right in zip(lefts, rights))
        result = jnp.where(keep, result.reshape(chunk, leaves, 128), 0.0)
        sums[start : start + chunk, :] = jnp.sum(result, 1)
    folded = sums[...]
    folded = folded + pltpu.roll(folded, 128 - leaves, 1) + pltpu.roll(folded, 128 - 2 * leaves, 1)
    lane = iota((coef, 128), 1)
    first, second, third = split3(folded)
    stacked = jnp.where(lane < leaves, first, 0.0)
    stacked = jnp.where(lane // leaves == 1, pltpu.roll(second, leaves, 1), stacked)
    stacked = jnp.where(lane // leaves == 2, pltpu.roll(third, 2 * leaves, 1), stacked)
    span = 128 // per_device
    row, col = iota((128, 128), 0), iota((128, 128), 1)
    slot = col % span
    wanted = child_leaf(col // span, slot // 3, cells) + leaves * (slot % 3)
    chosen = multiply(stacked, mask((row == wanted) & (slot < 24)))
    slot = lane % span
    result = jnp.zeros((coef, 128), jnp.float32)
    for octant in range(8):
        for j, left in enumerate(split3(upward[:, octant, :])):
            right = jnp.where((slot >= 3 * octant) & (slot < 3 * octant + 3 - j), chosen, 0.0)
            result = result + multiply(left, right)
    out[...] = narrow(jnp.sum(result.T.reshape(per_device, span, coef), 1))


def multipole(offsets, charge_live, upward):
    cells, width = charge_live.shape[:3], charge_live.shape[3]
    leaves = cells[0] * cells[1] * cells[2]
    coef = upward.shape[0]
    vmem = pl.BlockSpec(memory_space=pltpu.VMEM)
    return pl.pallas_call(
        functools.partial(multipole_body, cells),
        out_shape=jax.ShapeDtypeStruct((leaves // 8, coef), jnp.bfloat16),
        in_specs=[vmem] * 3,
        out_specs=vmem,
        scratch_shapes=[
            pltpu.VMEM((3, leaves, width), jnp.float32),
            pltpu.VMEM((leaves, width), jnp.float32),
            pltpu.VMEM((coef, leaves, width), jnp.float32),
            pltpu.VMEM((coef, 128), jnp.float32),
        ],
        name="multipole",
    )(offsets, charge_live, upward)


def translate_body(info, mine, counts, table, remote, offsets, near, downward, out, *scratch):
    cells, per_device, lists, wide = info
    matrix, weights, sums, flat, basis, spread_local, sem = scratch
    fetch = pltpu.make_async_copy(remote, matrix, sem)
    fetch.start()
    coef, _, ops = matrix.shape
    leaves, width = near.shape
    _, cells_y, cells_z = cells
    rows = table.shape[0]
    span = 128 // per_device
    blocks = -(-coef // span)
    chunk = next(n for n in range(11, 0, -1) if coef % n == 0)
    fill_basis(offsets, flat, basis)

    seg = 256
    head = table[:, 0:128].astype(jnp.float32)
    owned = head[:, coef : coef + 1] + 256.0 * head[:, coef + 1 : coef + 2]
    lane = iota((rows, 128), 1)
    chosen = mask((owned.astype(jnp.int32) == lane + mine[0]) & (lane < per_device))
    entries = multiply(chosen.T[0:8], table[:, 128 : 128 + wide * seg])
    sources = entries[:, seg : 2 * seg]
    if wide == 3:
        sources = sources + 256.0 * entries[:, 2 * seg : 3 * seg]
    sources = sources.astype(jnp.int32)
    classes = entries[:, 0:seg].astype(jnp.int32)
    across = (((1,), (1,)), ((), ()))
    counted = []
    for row in range(per_device):
        from_cell = mask(iota((rows, seg), 0) == sources[row : row + 1])
        to_class = iota((ops, seg), 0) == classes[row : row + 1]
        to_class = mask(to_class & (iota((ops, seg), 1) < lists))
        counted.append(narrow(multiply(to_class, from_cell, across)))
    counted = jnp.concatenate(counted, 1)
    parents = table[:, 0:128]
    for block in range(blocks):
        row, col = iota((128, 128), 0), iota((128, 128), 1)
        tiled = multiply(parents, mask((row == span * block + col % span) & (row < coef)))
        stacked = [jnp.where(lane // span == row, tiled, 0.0) for row in range(per_device)]
        weights[block] = narrow(multiply(counted, jnp.concatenate(stacked, 0)))
    fetch.wait()
    for start in range(0, coef, chunk):
        total = jnp.zeros((chunk, 128), jnp.float32)
        for block in range(blocks):
            height = min(span, coef - span * block)
            part = matrix[start : start + chunk, span * block : span * block + height, :]
            if height < span:
                fill = jnp.zeros((chunk, span - height, ops), part.dtype)
                part = jnp.concatenate([part, fill], 1)
            result = multiply(part.reshape(chunk * span, ops), weights[block])
            result = result.reshape(chunk, span, 128)
            keep = iota((chunk, span, 128), 1) == iota((chunk, span, 128), 2) % span
            total = total + jnp.sum(jnp.where(keep, result, 0.0), 1)
        sums[start : start + chunk, :] = total
    gather = mask(iota((128, 128), 0) // span == iota((128, 128), 1))
    local = sum(multiply(piece, gather) for piece in split3(sums[...]))
    local = jnp.concatenate(split3(local.T[0:8]), 0)
    for octant in range(8):
        result = jnp.zeros((8, coef), jnp.float32)
        for j, right in enumerate(split3(downward[:, octant, :])):
            product = multiply(local, right, across)
            for i in range(3 - j):
                result = result + product[8 * i : 8 * i + 8]
        for parent in range(per_device):
            leaf = child_leaf(parent, octant, cells)
            spread_local[leaf : leaf + 1, 0:coef] = result[parent : parent + 1]
    slot = iota((8, width), 1)
    sub = iota((8, width), 0)
    for first in range(0, leaves, 8):
        values = spread_local[first : first + 8, :]
        total = near[first : first + 8, :]
        for index in range(coef):
            column = jnp.broadcast_to(values[:, index : index + 1], (8, width))
            total = total + column * basis[index, first : first + 8, :]
        limit = jnp.zeros((8, width), jnp.int32)
        for row in range(8):
            leaf = first + row
            count = counts[leaf // (cells_y * cells_z), leaf // cells_z % cells_y, leaf % cells_z]
            limit = jnp.where(sub == row, count, limit)
        total = jnp.where(slot < limit, total, 0.0)
        for row in range(0, 8, cells_z):
            leaf = first + row
            a, b = leaf // (cells_y * cells_z), leaf // cells_z % cells_y
            out[a, b] = total[row : row + cells_z]


def translate(mine, counts, table, matrix, offsets, near, downward, lists, wide):
    cells = counts.shape
    coef, _, ops = matrix.shape
    leaves, width = near.shape
    per_device = leaves // 8
    span = 128 // per_device
    smem = pl.BlockSpec(memory_space=pltpu.SMEM)
    vmem = pl.BlockSpec(memory_space=pltpu.VMEM)
    return pl.pallas_call(
        functools.partial(translate_body, (cells, per_device, lists, wide)),
        out_shape=jax.ShapeDtypeStruct(cells + (width,), jnp.float32),
        in_specs=[smem, smem, vmem, pl.BlockSpec(memory_space=pl.ANY)] + [vmem] * 3,
        out_specs=vmem,
        scratch_shapes=[
            pltpu.VMEM(matrix.shape, matrix.dtype),
            pltpu.VMEM((-(-coef // span), ops, 128), jnp.bfloat16),
            pltpu.VMEM((coef, 128), jnp.float32),
            pltpu.VMEM((3, leaves, width), jnp.float32),
            pltpu.VMEM((coef, leaves, width), jnp.float32),
            pltpu.VMEM((leaves, 128), jnp.float32),
            pltpu.SemaphoreType.DMA(()),
        ],
        name="translate",
    )(mine, counts, table, matrix, offsets, near, downward)


MESH_AXES = ("gx", "gy", "gz")


def extended(value, sides):
    for axis, dim in sides:
        value = padded_along(value, axis, dim)
    return value


def padded_along(value, axis, dim):
    peers, length = lax.axis_size(axis), value.shape[dim]
    last = lax.slice_in_dim(value, length - 1, length, axis=dim)
    leading = lax.slice_in_dim(value, 0, 1, axis=dim)
    if peers == 2:
        upper = lax.axis_index(axis) == 1
        other = lax.ppermute(jnp.where(upper, leading, last), axis, [(0, 1), (1, 0)])
        before = jnp.where(upper, other, 0.0)
        after = jnp.where(upper, 0.0, other)
    else:
        up = [(i, i + 1) for i in range(peers - 1)]
        before = lax.ppermute(last, axis, up)
        after = lax.ppermute(leading, axis, [(j, i) for i, j in up])
    return jnp.concatenate([before, value, after], axis=dim)


def columns(cell, halves, peers):
    (half_x, half_y, half_z), (_, count_y, count_z) = halves, peers
    parents_y, parents_z = half_y * count_y, half_z * count_z
    cell_a = cell // (parents_y * parents_z)
    cell_b = cell // parents_z % parents_y
    cell_c = cell % parents_z
    device = (cell_a // half_x * count_y + cell_b // half_y) * count_z + cell_c // half_z
    local = (cell_a % half_x * half_y + cell_b % half_y) * half_z + cell_c % half_z
    return device * (half_x * half_y * half_z) + local


def per_block(offsets, charges, counts, owned_cell, list_sources, list_ops, m2m, m2l, l2l):
    cells = cells_x, cells_y, cells_z = charges.shape[:3]
    width = charges.shape[3]
    halves = half_x, half_y, half_z = (cells_x // 2, cells_y // 2, cells_z // 2)
    per_device = half_x * half_y * half_z
    peers = tuple(lax.axis_size(axis) for axis in MESH_AXES)
    devices = peers[0] * peers[1] * peers[2]
    total_parents = per_device * devices
    slot_ids = jnp.arange(width, dtype=jnp.int32)
    live = (slot_ids[None, None, None, :] < counts[..., None]).astype(jnp.float32)
    charge_live = charges * live
    stacked = jnp.concatenate([offsets, charge_live[None]], 0)
    padded = extended(stacked, (("gz", 3), ("gy", 2), ("gx", 1)))

    coef = m2m.shape[1]
    parent_rows = multipole(offsets, charge_live, m2m.transpose(1, 0, 2))

    lists = list_sources.shape[1]
    wide = 2 if total_parents <= 256 else 3
    owner_columns = columns(owned_cell, halves, peers)[:, None]
    source_columns = columns(list_sources, halves, peers)

    def segment(values, size):
        values = values.astype(jnp.bfloat16)
        return jnp.pad(values, ((0, 0), (0, size - values.shape[1])))

    pieces = [
        parent_rows,
        segment(owner_columns % 256, 1),
        segment(owner_columns // 256, 127 - coef),
        segment(list_ops, 256),
        segment(source_columns % 256, 256),
    ]
    if wide == 3:
        pieces.append(segment(source_columns // 256, 256))
    payload = jnp.concatenate(pieces, 1)
    spread = jnp.broadcast_to(payload[None], (devices,) + payload.shape)
    table = lax.all_to_all(spread, MESH_AXES, 0, 0)
    table = table.reshape(total_parents, payload.shape[1])

    near = near_field(counts, padded, cells)
    mine = (lax.axis_index(MESH_AXES) * per_device).astype(jnp.int32).reshape(1)
    downward = l2l.transpose(1, 0, 2)
    return translate(mine, counts, table, m2l, offsets, near, downward, lists, wide)


def solution(mesh):
    placed = (
        P(None, "gx", "gy", "gz", None),
        P("gx", "gy", "gz", None),
        P("gx", "gy", "gz"),
        P(("gx", "gy", "gz")),
        P(("gx", "gy", "gz"), None),
        P(("gx", "gy", "gz"), None),
        P(),
        P(),
        P(),
    )
    return jax.shard_map(
        per_block, mesh=mesh, in_specs=placed, out_specs=P("gx", "gy", "gz", None), check_vma=False
    )
```

```python
import math
import functools
import numpy as np
import jax
import jax.numpy as jnp
from jax import lax
from jax.experimental import pallas as pl
from jax.experimental.pallas import tpu as pltpu
from jax.sharding import PartitionSpec as P


ORDER = 10
SOFTENING = 0.01
DELTAS = [(dx, dy, dz) for dx in (-1, 0, 1) for dy in (-1, 0, 1) for dz in (-1, 0, 1)]
DEPTH = 80


def delta_rows(delta):
    row = iota((32, 128), 0)
    values = jnp.zeros((32, 128), jnp.float32)
    for axis in range(3):
        values = jnp.where((row < 9) & (row % 3 == axis), 2.0 * delta[axis], values)
        values = jnp.where((row >= 16) & (row < 25) & (row % 3 == (axis + 1) % 3), delta[axis], values)
    rest = np.float32(sum(d * d for d in delta) + SOFTENING)
    for part in range(3):
        piece = np.asarray(rest).astype(jnp.bfloat16).astype(np.float32)
        values = jnp.where(row == 25 + part, float(piece), values)
        rest = np.float32(rest - piece)
    return values


def expand_rows():
    row, col = iota((32, 128), 0), iota((32, 128), 1)
    slot = col % 16
    triple, axis = slot // 3, slot % 3
    field = col // 16
    known = slot < 9
    product = (field < 3) & known & (triple < 3 - field) & (row == 3 * field + axis)
    offset = (field == 4) & known & (row == slot)
    plain = (field == 0) & (slot >= 9) & (slot < 12) & (row == 12)
    norm = (field == 0) & (slot >= 12) & (slot < 15) & (row == slot - 3)
    shift = (field == 3) & known & (row == 12)
    rest = (field == 4) & (slot >= 9) & (slot < 12) & (row == 12)
    values = jnp.where(product | offset, -2.0, 0.0)
    return jnp.where(plain | norm | shift | rest, 1.0, values)


def split3(value):
    first = value.astype(jnp.bfloat16).astype(jnp.float32)
    rest = value - first
    second = rest.astype(jnp.bfloat16).astype(jnp.float32)
    third = (rest - second).astype(jnp.bfloat16).astype(jnp.float32)
    return first, second, third


def iota(shape, dim):
    return lax.broadcasted_iota(jnp.int32, shape, dim)


def mask(condition):
    return jnp.where(condition, 1.0, 0.0)


def narrow(value):
    return value.astype(jnp.bfloat16)


def multiply(left, right, dims=(((1,), (0,)), ((), ()))):
    return lax.dot_general(narrow(left), narrow(right), dims, preferred_element_type=jnp.float32)


def near_body(cells, counts, lower, middle, upper, out, rows32, base, left, total, table):
    cells_x, cells_y, cells_z = cells
    _, _, pad_y, pad_z, width = middle.shape
    pad_x = cells_x + 2
    leaves = cells_x * cells_y * cells_z
    tiles = width // 128
    sources = pad_x * pad_y * pad_z

    def fill(source, first, place, carry):
        a, b = place // pad_y, place % pad_y
        column = first * pad_y + place
        parts, norm = [], 0.0
        for axis in range(3):
            centred = source[axis, a, b] - 0.5
            norm = norm + centred * centred
            parts.append(split3(centred))
        rows = [parts[axis][part] for part in range(3) for axis in range(3)]
        rows += list(split3(norm)) + [jnp.ones_like(norm)] * 3 + [source[3, a, b]]
        for index, row in enumerate(rows):
            for part in range(tiles):
                start = part * sources * 16 + column * pad_z * 16 + index
                rows32[pl.ds(start, pad_z, stride=16), :] = row[:, 128 * part : 128 * part + 128]
        return carry

    def pack(leaf, carry):
        for part in range(tiles):
            start = pl.multiple_of((part * sources + leaf) * 16, 16)
            base[leaf, :, 128 * part : 128 * part + 128] = narrow(rows32[pl.ds(start, 16), :])
        return carry

    for index, delta in enumerate(DELTAS):
        table[index] = narrow(delta_rows(delta))
    table[len(DELTAS)] = narrow(expand_rows())
    for source, first in ((lower, 0), (middle, 1), (upper, cells_x + 1)):
        columns = source.shape[1] * pad_y
        lax.fori_loop(0, columns, functools.partial(fill, source, first), 0, unroll=2)
    lax.fori_loop(0, pad_x * pad_y * pad_z, pack, 0, unroll=8)

    def place(leaf):
        return leaf // (cells_y * cells_z), leaf // cells_z % cells_y, leaf % cells_z

    def home(leaf):
        a, b, c = place(leaf)
        return ((a + 1) * pad_y + b + 1) * pad_z + c + 1

    def count_of(leaf):
        a, b, c = place(leaf)
        return counts[a, b, c]

    def fill_left(leaf):
        features = base[home(leaf)].astype(jnp.float32).T
        left[leaf % 2] = narrow(multiply(features, table[len(DELTAS), 0:16]))

    ones = jnp.ones((8, 128), jnp.bfloat16)
    across = (((1,), (1,)), ((), ()))

    def finish(leaf):
        result = sum(multiply(ones, piece, across) for piece in split3(total[leaf % 2]))
        slot = iota((1, width), 1)
        out[pl.ds(leaf, 1), :] = jnp.where(slot < count_of(leaf), result[0:1], 0.0)

    def block(leaf, height):
        centre = home(leaf)
        lhs = left[leaf % 2, 0:height, 0:DEPTH]
        acc = jnp.zeros((height, 128), jnp.float32)
        for index, (dx, dy, dz) in enumerate(DELTAS):
            other = centre + (dx * pad_y + dy) * pad_z + dz
            scale = table[index, 0:16]
            fixed = table[index, 16:32]
            halves = []
            for part in range(tiles):
                feature = base[other, :, 128 * part : 128 * part + 128]
                halves.append(
                    jnp.concatenate([feature, feature, feature, feature * scale, fixed], 0)
                )
            rhs = jnp.concatenate(halves, 1)
            dist2 = jnp.dot(lhs, rhs, preferred_element_type=jnp.float32)
            inverse = lax.rsqrt(dist2)
            if dx == 0 and dy == 0 and dz == 0:
                inverse = jnp.where(iota(inverse.shape, 0) == iota(inverse.shape, 1), 0.0, inverse)
            for part in range(tiles):
                amount = rows32[pl.ds((part * sources + other) * 16 + 15, 1), :]
                acc = acc + inverse[:, 128 * part : 128 * part + 128] * amount
        fill_left(jnp.minimum(leaf + 1, leaves - 1))
        finish(jnp.maximum(leaf - 1, 0))
        total[leaf % 2, 0:height] = acc

    fill_left(0)
    total[...] = jnp.zeros_like(total)
    step = 32

    def choose(leaf, pieces, low, high):
        if high - low == 1:
            block(leaf, high * step)
            return
        middle = (low + high) // 2
        pl.when(pieces <= middle)(lambda: choose(leaf, pieces, low, middle))
        pl.when(pieces > middle)(lambda: choose(leaf, pieces, middle, high))

    def leaf_step(leaf, carry):
        pieces = (count_of(leaf) + step - 1) // step
        choose(leaf, pieces, 0, width // step)
        return carry

    lax.fori_loop(0, leaves, leaf_step, 0)
    finish(leaves - 1)


def near_field(counts, slabs, cells):
    leaves = cells[0] * cells[1] * cells[2]
    width = slabs[1].shape[-1]
    sources = (cells[0] + 2) * slabs[1].shape[2] * slabs[1].shape[3]
    vmem = pl.BlockSpec(memory_space=pltpu.VMEM)
    return pl.pallas_call(
        functools.partial(near_body, cells),
        out_shape=jax.ShapeDtypeStruct((leaves, width), jnp.float32),
        in_specs=[pl.BlockSpec(memory_space=pltpu.SMEM)] + [vmem] * 3,
        out_specs=vmem,
        scratch_shapes=[
            pltpu.VMEM((sources * 16 * (width // 128), 128), jnp.float32),
            pltpu.VMEM((sources, 16, width), jnp.bfloat16),
            pltpu.VMEM((2, width, 128), jnp.bfloat16),
            pltpu.VMEM((2, width, 128), jnp.float32),
            pltpu.VMEM((len(DELTAS) + 1, 32, 128), jnp.bfloat16),
        ],
        cost_estimate=pl.CostEstimate(
            flops=leaves * 27 * width * width * 2 * DEPTH,
            transcendentals=leaves * 27 * width * width,
            bytes_accessed=sources * 4 * width * 4,
        ),
        compiler_params=pltpu.CompilerParams(vmem_limit_bytes=24 << 20),
        name="near",
    )(counts, *slabs)


def emit_harmonics(coord_x, coord_y, coord_z, emit):
    radius2 = coord_x * coord_x + coord_y * coord_y + coord_z * coord_z

    def give(degree, azimuth, real, imag):
        if azimuth == 0:
            emit(degree * degree, real)
        else:
            emit(degree * degree + 2 * azimuth - 1, real)
            emit(degree * degree + 2 * azimuth, imag)

    top_re, top_im = jnp.ones_like(coord_x), None
    for azimuth in range(ORDER + 1):
        if azimuth == 1:
            top_re, top_im = coord_x, coord_y
        elif azimuth > 1:
            factor = math.sqrt((2 * azimuth - 1) / (2 * azimuth))
            top_re, top_im = (
                factor * (coord_x * top_re - coord_y * top_im),
                factor * (coord_x * top_im + coord_y * top_re),
            )
        give(azimuth, azimuth, top_re, top_im)
        older, newer = None, (top_re, top_im)
        for degree in range(azimuth + 1, ORDER + 1):
            denom = math.sqrt(degree * degree - azimuth * azimuth)
            scaled = ((2 * degree - 1) / denom) * coord_z
            lower = None
            if degree - 2 >= azimuth:
                lower = (math.sqrt((degree - 1) ** 2 - azimuth * azimuth) / denom) * radius2
            values = []
            for part in range(1 if azimuth == 0 else 2):
                value = scaled * newer[part]
                if lower is not None:
                    value = value - lower * older[part]
                values.append(value)
            older, newer = newer, tuple(values)
            give(degree, azimuth, values[0], values[-1])


def flatten(field, flat):
    size_x, size_y, size_z = field.shape[:3]
    for a in range(size_x):
        for b in range(size_y):
            first = (a * size_y + b) * size_z
            flat[first : first + size_z, :] = field[a, b]


def flatten_children(field, flat, cells):
    _, cells_y, cells_z = cells
    for parent in range(flat.shape[0] // 8):
        for octant in range(0, 8, 2):
            leaf = child_leaf(parent, octant, cells)
            a, b, c = leaf // (cells_y * cells_z), leaf // cells_z % cells_y, leaf % cells_z
            first = 8 * parent + octant
            flat[first : first + 2, :] = field[a, b, c : c + 2]


def fill_basis(offsets, flat, basis, cells=None):
    leaves = flat.shape[1]
    for axis in range(3):
        if cells:
            flatten_children(offsets.at[axis], flat.at[axis], cells)
        else:
            flatten(offsets.at[axis], flat.at[axis])
    for first in range(0, leaves, 8):
        rows = slice(first, first + 8)
        x, y, z = (flat[axis, rows, :] - 0.5 for axis in range(3))

        def emit(index, value):
            basis[index, rows, :] = value

        emit_harmonics(x, y, z, emit)


def child_leaf(parent, octant, cells):
    _, cells_y, cells_z = cells
    half_y, half_z = cells_y // 2, cells_z // 2
    a = parent // (half_y * half_z)
    b = parent // half_z % half_y
    c = parent % half_z
    x = 2 * a + octant // 4
    y = 2 * b + octant // 2 % 2
    z = 2 * c + octant % 2
    return (x * cells_y + y) * cells_z + z


def limits(counts, first, size, width):
    _, size_y, size_z = counts.shape
    rows = iota((size, width), 0)
    limit = jnp.zeros((size, width), jnp.int32)
    for row in range(size):
        leaf = first + row
        count = counts[leaf // (size_y * size_z), leaf // size_z % size_y, leaf % size_z]
        limit = jnp.where(rows == row, count, limit)
    return limit


def over(value, divisor):
    return jnp.floor((value + 0.5) * (1.0 / divisor))


def columns(cell, halves, peers):
    (half_x, half_y, half_z), (_, count_y, count_z) = halves, peers
    parents_y, parents_z = half_y * count_y, half_z * count_z
    cell_a = over(cell, parents_y * parents_z)
    rest = cell - cell_a * (parents_y * parents_z)
    cell_b = over(rest, parents_z)
    cell_c = rest - cell_b * parents_z
    device, local = 0.0, 0.0
    for part, half, count in zip((cell_a, cell_b, cell_c), halves, peers):
        owner = over(part, half)
        device = device * count + owner
        local = local * half + (part - owner * half)
    return device * (half_x * half_y * half_z) + local


def multipole_body(info, counts, owned, offsets, charges, upward, sources, classes, out, *scratch):
    cells, peers, wide = info
    flat, charge, basis, sums = scratch
    leaves, width = charge.shape
    coef = upward.shape[0]
    per_device = leaves // 8
    halves = tuple(size // 2 for size in cells)
    flatten(charges, charge)
    for first in range(0, leaves, 8):
        live = iota((8, width), 1) < limits(counts, first, 8, width)
        charge[first : first + 8, :] = jnp.where(live, charge[first : first + 8, :], 0.0)
    fill_basis(offsets, flat, basis)
    parts = jnp.concatenate(split3(charge[...]) + (jnp.zeros((128 - 3 * leaves, width)),), 0)
    columns_all = parts.T
    lane = iota((width, 128), 1)
    chunk = next(n for n in range(11, 0, -1) if coef % n == 0)
    rights = [narrow(jnp.where(lane < leaves * (3 - j), columns_all, 0.0)) for j in range(3)]
    keep = iota((chunk, leaves, 128), 1) == iota((chunk, leaves, 128), 2) % leaves
    for start in range(0, coef, chunk):
        lefts = split3(basis[start : start + chunk].reshape(chunk * leaves, width))
        result = sum(multiply(left, right) for left, right in zip(lefts, rights))
        result = jnp.where(keep, result.reshape(chunk, leaves, 128), 0.0)
        sums[start : start + chunk, :] = jnp.sum(result, 1)
    folded = sums[...]
    folded = folded + pltpu.roll(folded, 128 - leaves, 1) + pltpu.roll(folded, 128 - 2 * leaves, 1)
    lane = iota((coef, 128), 1)
    first, second, third = split3(folded)
    stacked = jnp.where(lane < leaves, first, 0.0)
    stacked = jnp.where(lane // leaves == 1, pltpu.roll(second, leaves, 1), stacked)
    stacked = jnp.where(lane // leaves == 2, pltpu.roll(third, 2 * leaves, 1), stacked)
    span = 128 // per_device
    row, col = iota((128, 128), 0), iota((128, 128), 1)
    slot = col % span
    wanted = child_leaf(col // span, slot // 3, cells) + leaves * (slot % 3)
    chosen = multiply(stacked, mask((row == wanted) & (slot < 24)))
    slot = lane % span
    result = jnp.zeros((coef * 8, 128), jnp.float32)
    for j, left in enumerate(split3(upward[...].reshape(coef * 8, coef))):
        result = result + multiply(left, jnp.where(slot % 3 < 3 - j, chosen, 0.0))
    shape = (coef, 8, 128)
    result = jnp.where(iota(shape, 1) == iota(shape, 2) % span // 3, result.reshape(shape), 0.0)
    parent = jnp.sum(jnp.sum(result, 1).T.reshape(per_device, span, coef), 1)

    def wider(value, size):
        fill = jnp.zeros((per_device, size - value.shape[1]), jnp.float32)
        return jnp.concatenate([value, fill], 1)

    shape = (per_device, 128)
    cell = jnp.zeros(shape, jnp.float32)
    for row in range(per_device):
        cell = jnp.where(iota(shape, 0) == row, owned[row].astype(jnp.float32), cell)
    column = columns(cell, halves, peers)
    upper = over(column, 256)
    head = wider(parent, 128)
    head = jnp.where(iota(shape, 1) == coef, column - 256.0 * upper, head)
    head = jnp.where(iota(shape, 1) == coef + 1, upper, head)
    column = columns(sources[...].astype(jnp.float32), halves, peers)
    upper = over(column, 256)
    pieces = [head, wider(classes[...].astype(jnp.float32), 256)]
    pieces.append(wider(column - 256.0 * upper, 256))
    if wide == 3:
        pieces.append(wider(upper, 256))
    payload = narrow(jnp.concatenate(pieces, 1))

    def spread(device, carry):
        out[device] = payload
        return carry

    lax.fori_loop(0, out.shape[0], spread, 0, unroll=8)


def multipole(counts, owned, offsets, charges, upward, sources, classes, peers, wide):
    cells, width = charges.shape[:3], charges.shape[3]
    leaves = cells[0] * cells[1] * cells[2]
    coef = upward.shape[0]
    devices = peers[0] * peers[1] * peers[2]
    smem = pl.BlockSpec(memory_space=pltpu.SMEM)
    vmem = pl.BlockSpec(memory_space=pltpu.VMEM)
    return pl.pallas_call(
        functools.partial(multipole_body, (cells, peers, wide)),
        out_shape=jax.ShapeDtypeStruct((devices, leaves // 8, 128 + 256 * wide), jnp.bfloat16),
        in_specs=[smem, smem] + [vmem] * 5,
        out_specs=vmem,
        scratch_shapes=[
            pltpu.VMEM((3, leaves, width), jnp.float32),
            pltpu.VMEM((leaves, width), jnp.float32),
            pltpu.VMEM((coef, leaves, width), jnp.float32),
            pltpu.VMEM((coef, 128), jnp.float32),
        ],
        name="multipole",
    )(counts, owned, offsets, charges, upward, sources, classes)


FETCHES = 11


def translate_body(info, mine, counts, arrived, remote, offsets, near, downward, out, *scratch):
    cells, per_device, lists, wide = info
    table, matrix, weights, sums, flat, basis, spread_local, sem = scratch
    coef, _, ops = matrix.shape
    chunk = next(n for n in range(11, 0, -1) if coef % n == 0)
    fetches = []
    for start in range(0, coef, chunk):
        window = pl.ds(start, chunk)
        copy = pltpu.make_async_copy(remote.at[window], matrix.at[window], sem.at[start // chunk])
        copy.start()
        fetches.append(copy)
    _, width = near.shape
    _, cells_y, cells_z = cells
    rows = table.shape[0]
    span = 128 // per_device
    blocks = -(-coef // span)
    fill_basis(offsets, flat, basis, cells)
    group = 8 // per_device

    def settle(index, carry):
        rows = [arrived[index * group + part].astype(jnp.float32) for part in range(group)]
        table[pl.ds(pl.multiple_of(8 * index, 8), 8), :] = jnp.concatenate(rows, 0)
        return carry

    lax.fori_loop(0, arrived.shape[0] // group, settle, 0, unroll=4)

    seg = 256
    head = table[:, 0:128]
    owned = head[:, coef : coef + 1] + 256.0 * head[:, coef + 1 : coef + 2]
    lane = iota((rows, 128), 1)
    chosen = mask((owned.astype(jnp.int32) == lane + mine[0]) & (lane < per_device))
    entries = multiply(chosen.T[0:8], table[:, 128 : 128 + wide * seg])
    sources = entries[:, seg : 2 * seg]
    if wide == 3:
        sources = sources + 256.0 * entries[:, 2 * seg : 3 * seg]
    sources = sources.astype(jnp.int32)
    classes = entries[:, 0:seg].astype(jnp.int32)
    across = (((1,), (1,)), ((), ()))
    counted = []
    for row in range(per_device):
        from_cell = mask(iota((rows, seg), 0) == sources[row : row + 1])
        to_class = iota((ops, seg), 0) == classes[row : row + 1]
        to_class = mask(to_class & (iota((ops, seg), 1) < lists))
        counted.append(narrow(multiply(to_class, from_cell, across)))
    counted = jnp.concatenate(counted, 1)
    parents = table[:, 0:128]
    for block in range(blocks):
        row, col = iota((128, 128), 0), iota((128, 128), 1)
        tiled = multiply(parents, mask((row == span * block + col % span) & (row < coef)))
        stacked = [jnp.where(lane // span == row, tiled, 0.0) for row in range(per_device)]
        weights[block] = narrow(multiply(counted, jnp.concatenate(stacked, 0)))
    for start in range(0, coef, chunk):
        if start // chunk % FETCHES == 0:
            for copy in fetches[start // chunk : start // chunk + FETCHES]:
                copy.wait()
        total = jnp.zeros((chunk, 128), jnp.float32)
        for block in range(blocks):
            height = min(span, coef - span * block)
            part = matrix[start : start + chunk, span * block : span * block + height, :]
            if height < span:
                fill = jnp.zeros((chunk, span - height, ops), part.dtype)
                part = jnp.concatenate([part, fill], 1)
            result = multiply(part.reshape(chunk * span, ops), weights[block])
            result = result.reshape(chunk, span, 128)
            keep = iota((chunk, span, 128), 1) == iota((chunk, span, 128), 2) % span
            total = total + jnp.sum(jnp.where(keep, result, 0.0), 1)
        sums[start : start + chunk, :] = total
    gather = mask(iota((128, 128), 0) // span == iota((128, 128), 1))
    local = sum(multiply(piece, gather) for piece in split3(sums[...]))
    parts = split3(local)
    result = jnp.zeros((coef * 8, 128), jnp.float32)
    for j, left in enumerate(split3(downward[...].reshape(coef * 8, coef))):
        for right in parts[0 : 3 - j]:
            result = result + multiply(left, right)
    spread_local[...] = result
    for parent in range(per_device):
        rows = slice(8 * parent, 8 * parent + 8)
        total = jnp.zeros((8, width), jnp.float32)
        for index in range(coef):
            values = spread_local[8 * index : 8 * index + 8, parent : parent + 1]
            total = total + jnp.broadcast_to(values, (8, width)) * basis[index, rows, :]
        for octant in range(0, 8, 2):
            leaf = child_leaf(parent, octant, cells)
            a, b, c = leaf // (cells_y * cells_z), leaf // cells_z % cells_y, leaf % cells_z
            limit = jnp.zeros((2, width), jnp.int32)
            for row in range(2):
                limit = jnp.where(iota((2, width), 0) == row, counts[a, b, c + row], limit)
            value = total[octant : octant + 2] + near[leaf : leaf + 2, :]
            out[a, b, c : c + 2, :] = jnp.where(iota((2, width), 1) < limit, value, 0.0)


def translate(mine, counts, table, matrix, offsets, near, downward, lists, wide):
    cells = counts.shape
    coef, _, ops = matrix.shape
    leaves, width = near.shape
    per_device = leaves // 8
    span = 128 // per_device
    smem = pl.BlockSpec(memory_space=pltpu.SMEM)
    vmem = pl.BlockSpec(memory_space=pltpu.VMEM)
    return pl.pallas_call(
        functools.partial(translate_body, (cells, per_device, lists, wide)),
        out_shape=jax.ShapeDtypeStruct(cells + (width,), jnp.float32),
        in_specs=[smem, smem, vmem, pl.BlockSpec(memory_space=pl.ANY)] + [vmem] * 3,
        out_specs=vmem,
        scratch_shapes=[
            pltpu.VMEM((table.shape[0] * table.shape[1], table.shape[2]), jnp.float32),
            pltpu.VMEM(matrix.shape, matrix.dtype),
            pltpu.VMEM((-(-coef // span), ops, 128), jnp.bfloat16),
            pltpu.VMEM((coef, 128), jnp.float32),
            pltpu.VMEM((3, leaves, width), jnp.float32),
            pltpu.VMEM((coef, leaves, width), jnp.float32),
            pltpu.VMEM((8 * coef, 128), jnp.float32),
            pltpu.SemaphoreType.DMA((coef,)),
        ],
        name="translate",
    )(mine, counts, table, matrix, offsets, near, downward)


MESH_AXES = ("gx", "gy", "gz")


def padded_along(value, axis, dim):
    peers, length = lax.axis_size(axis), value.shape[dim]
    last = lax.slice_in_dim(value, length - 1, length, axis=dim)
    leading = lax.slice_in_dim(value, 0, 1, axis=dim)
    if peers == 2:
        upper = lax.axis_index(axis) == 1
        other = lax.ppermute(jnp.where(upper, leading, last), axis, [(0, 1), (1, 0)])
        before = jnp.where(upper, other, 0.0)
        after = jnp.where(upper, 0.0, other)
    else:
        up = [(i, i + 1) for i in range(peers - 1)]
        before = lax.ppermute(last, axis, up)
        after = lax.ppermute(leading, axis, [(j, i) for i, j in up])
    return before, value, after


def per_block(offsets, charges, counts, owned_cell, list_sources, list_ops, m2m, m2l, l2l):
    cells = charges.shape[:3]
    per_device = cells[0] * cells[1] * cells[2] // 8
    peers = tuple(lax.axis_size(axis) for axis in MESH_AXES)
    total_parents = per_device * peers[0] * peers[1] * peers[2]
    slot_ids = jnp.arange(charges.shape[3], dtype=jnp.int32)
    charge_live = jnp.where(slot_ids[None, None, None, :] < counts[..., None], charges, 0.0)
    padded = jnp.concatenate([offsets, charge_live[None]], 0)
    for axis, dim in (("gz", 3), ("gy", 2)):
        padded = jnp.concatenate(padded_along(padded, axis, dim), dim)
    slabs = padded_along(padded, "gx", 1)

    wide = 2 if total_parents <= 256 else 3
    upward = m2m.transpose(1, 0, 2)
    spread = multipole(
        counts, owned_cell, offsets, charges, upward, list_sources, list_ops, peers, wide
    )
    table = lax.all_to_all(spread, MESH_AXES, 0, 0)

    near = near_field(counts, slabs, cells)
    mine = (lax.axis_index(MESH_AXES) * per_device).astype(jnp.int32).reshape(1)
    downward = l2l.transpose(1, 0, 2)
    lists = list_sources.shape[1]
    return translate(mine, counts, table, m2l, offsets, near, downward, lists, wide)


def solution(mesh):
    placed = (
        P(None, "gx", "gy", "gz", None),
        P("gx", "gy", "gz", None),
        P("gx", "gy", "gz"),
        P(("gx", "gy", "gz")),
        P(("gx", "gy", "gz"), None),
        P(("gx", "gy", "gz"), None),
        P(),
        P(),
        P(),
    )
    return jax.shard_map(
        per_block, mesh=mesh, in_specs=placed, out_specs=P("gx", "gy", "gz", None), check_vma=False
    )
```

```python
import math
import functools
import numpy as np
import jax
import jax.numpy as jnp
from jax import lax
from jax.experimental import pallas as pl
from jax.experimental.pallas import tpu as pltpu
from jax.sharding import PartitionSpec as P


ORDER = 10
SOFTENING = 0.01
DELTAS = [(dx, dy, dz) for dx in (-1, 0, 1) for dy in (-1, 0, 1) for dz in (-1, 0, 1)]
DEPTH = 80


def delta_rows(delta):
    row = iota((32, 128), 0)
    values = jnp.zeros((32, 128), jnp.float32)
    for axis in range(3):
        values = jnp.where((row < 9) & (row % 3 == axis), 2.0 * delta[axis], values)
        values = jnp.where((row >= 16) & (row < 25) & (row % 3 == (axis + 1) % 3), delta[axis], values)
    rest = np.float32(sum(d * d for d in delta) + SOFTENING)
    for part in range(3):
        piece = np.asarray(rest).astype(jnp.bfloat16).astype(np.float32)
        values = jnp.where(row == 25 + part, float(piece), values)
        rest = np.float32(rest - piece)
    return values


def expand_rows():
    row, col = iota((32, 128), 0), iota((32, 128), 1)
    slot = col % 16
    triple, axis = slot // 3, slot % 3
    field = col // 16
    known = slot < 9
    product = (field < 3) & known & (triple < 3 - field) & (row == 3 * field + axis)
    offset = (field == 4) & known & (row == slot)
    plain = (field == 0) & (slot >= 9) & (slot < 12) & (row == 12)
    norm = (field == 0) & (slot >= 12) & (slot < 15) & (row == slot - 3)
    shift = (field == 3) & known & (row == 12)
    rest = (field == 4) & (slot >= 9) & (slot < 12) & (row == 12)
    values = jnp.where(product | offset, -2.0, 0.0)
    return jnp.where(plain | norm | shift | rest, 1.0, values)


def split3(value):
    first = value.astype(jnp.bfloat16).astype(jnp.float32)
    rest = value - first
    second = rest.astype(jnp.bfloat16).astype(jnp.float32)
    third = (rest - second).astype(jnp.bfloat16).astype(jnp.float32)
    return first, second, third


def iota(shape, dim):
    return lax.broadcasted_iota(jnp.int32, shape, dim)


def mask(condition):
    return jnp.where(condition, 1.0, 0.0)


def narrow(value):
    return value.astype(jnp.bfloat16)


def multiply(left, right, dims=(((1,), (0,)), ((), ()))):
    return lax.dot_general(narrow(left), narrow(right), dims, preferred_element_type=jnp.float32)


def near_body(cells, counts, lower, middle, upper, out, rows32, base, left, total, table):
    cells_x, cells_y, cells_z = cells
    _, _, pad_y, pad_z, width = middle.shape
    pad_x = cells_x + 2
    leaves = cells_x * cells_y * cells_z
    tiles = width // 128
    sources = pad_x * pad_y * pad_z

    def fill(source, first, place, carry):
        a, b = place // pad_y, place % pad_y
        column = first * pad_y + place
        parts, norm = [], 0.0
        for axis in range(3):
            centred = source[axis, a, b] - 0.5
            norm = norm + centred * centred
            parts.append(split3(centred))
        rows = [parts[axis][part] for part in range(3) for axis in range(3)]
        rows += list(split3(norm)) + [jnp.ones_like(norm)] * 3 + [source[3, a, b]]
        for index, row in enumerate(rows):
            for part in range(tiles):
                start = part * sources * 16 + column * pad_z * 16 + index
                rows32[pl.ds(start, pad_z, stride=16), :] = row[:, 128 * part : 128 * part + 128]
        return carry

    def pack(leaf, carry):
        for part in range(tiles):
            start = pl.multiple_of((part * sources + leaf) * 16, 16)
            base[leaf, :, 128 * part : 128 * part + 128] = narrow(rows32[pl.ds(start, 16), :])
        return carry

    for index, delta in enumerate(DELTAS):
        table[index] = narrow(delta_rows(delta))
    table[len(DELTAS)] = narrow(expand_rows())
    for source, first in ((lower, 0), (middle, 1), (upper, cells_x + 1)):
        columns = source.shape[1] * pad_y
        lax.fori_loop(0, columns, functools.partial(fill, source, first), 0, unroll=6)
    lax.fori_loop(0, pad_x * pad_y * pad_z, pack, 0, unroll=18)

    def place(leaf):
        return leaf // (cells_y * cells_z), leaf // cells_z % cells_y, leaf % cells_z

    def home(leaf):
        a, b, c = place(leaf)
        return ((a + 1) * pad_y + b + 1) * pad_z + c + 1

    def count_of(leaf):
        a, b, c = place(leaf)
        return counts[a, b, c]

    def fill_left(leaf):
        features = base[home(leaf)].astype(jnp.float32).T
        left[leaf % 2] = narrow(multiply(features, table[len(DELTAS), 0:16]))

    ones = jnp.ones((8, 128), jnp.bfloat16)
    across = (((1,), (1,)), ((), ()))

    def finish(leaf):
        result = sum(multiply(ones, piece, across) for piece in split3(total[leaf % 2]))
        slot = iota((1, width), 1)
        out[pl.ds(leaf, 1), :] = jnp.where(slot < count_of(leaf), result[0:1], 0.0)

    def block(leaf, height):
        centre = home(leaf)
        lhs = left[leaf % 2, 0:height, 0:DEPTH]
        acc = jnp.zeros((height, 128), jnp.float32)
        for index, (dx, dy, dz) in enumerate(DELTAS):
            other = centre + (dx * pad_y + dy) * pad_z + dz
            scale = table[index, 0:16]
            fixed = table[index, 16:32]
            halves = []
            for part in range(tiles):
                feature = base[other, :, 128 * part : 128 * part + 128]
                halves.append(
                    jnp.concatenate([feature, feature, feature, feature * scale, fixed], 0)
                )
            rhs = jnp.concatenate(halves, 1)
            dist2 = jnp.dot(lhs, rhs, preferred_element_type=jnp.float32)
            inverse = lax.rsqrt(dist2)
            if dx == 0 and dy == 0 and dz == 0:
                inverse = jnp.where(iota(inverse.shape, 0) == iota(inverse.shape, 1), 0.0, inverse)
            for part in range(tiles):
                amount = rows32[pl.ds((part * sources + other) * 16 + 15, 1), :]
                acc = acc + inverse[:, 128 * part : 128 * part + 128] * amount
        fill_left(jnp.minimum(leaf + 1, leaves - 1))
        finish(jnp.maximum(leaf - 1, 0))
        total[leaf % 2, 0:height] = acc

    fill_left(0)
    total[...] = jnp.zeros_like(total)
    step = 32

    def choose(leaf, pieces, low, high):
        if high - low == 1:
            block(leaf, high * step)
            return
        middle = (low + high) // 2
        pl.when(pieces <= middle)(lambda: choose(leaf, pieces, low, middle))
        pl.when(pieces > middle)(lambda: choose(leaf, pieces, middle, high))

    def leaf_step(leaf, carry):
        pieces = (count_of(leaf) + step - 1) // step
        choose(leaf, pieces, 0, width // step)
        return carry

    lax.fori_loop(0, leaves, leaf_step, 0)
    finish(leaves - 1)


def near_field(counts, slabs, cells):
    leaves = cells[0] * cells[1] * cells[2]
    width = slabs[1].shape[-1]
    sources = (cells[0] + 2) * slabs[1].shape[2] * slabs[1].shape[3]
    vmem = pl.BlockSpec(memory_space=pltpu.VMEM)
    return pl.pallas_call(
        functools.partial(near_body, cells),
        out_shape=jax.ShapeDtypeStruct((leaves, width), jnp.float32),
        in_specs=[pl.BlockSpec(memory_space=pltpu.SMEM)] + [vmem] * 3,
        out_specs=vmem,
        scratch_shapes=[
            pltpu.VMEM((sources * 16 * (width // 128), 128), jnp.float32),
            pltpu.VMEM((sources, 16, width), jnp.bfloat16),
            pltpu.VMEM((2, width, 128), jnp.bfloat16),
            pltpu.VMEM((2, width, 128), jnp.float32),
            pltpu.VMEM((len(DELTAS) + 1, 32, 128), jnp.bfloat16),
        ],
        cost_estimate=pl.CostEstimate(
            flops=leaves * 27 * width * width * 2 * DEPTH,
            transcendentals=leaves * 27 * width * width,
            bytes_accessed=sources * 4 * width * 4,
        ),
        compiler_params=pltpu.CompilerParams(vmem_limit_bytes=24 << 20),
        name="near",
    )(counts, *slabs)


def emit_harmonics(coord_x, coord_y, coord_z, emit):
    radius2 = coord_x * coord_x + coord_y * coord_y + coord_z * coord_z

    def give(degree, azimuth, real, imag):
        if azimuth == 0:
            emit(degree * degree, real)
        else:
            emit(degree * degree + 2 * azimuth - 1, real)
            emit(degree * degree + 2 * azimuth, imag)

    top_re, top_im = jnp.ones_like(coord_x), None
    for azimuth in range(ORDER + 1):
        if azimuth == 1:
            top_re, top_im = coord_x, coord_y
        elif azimuth > 1:
            factor = math.sqrt((2 * azimuth - 1) / (2 * azimuth))
            top_re, top_im = (
                factor * (coord_x * top_re - coord_y * top_im),
                factor * (coord_x * top_im + coord_y * top_re),
            )
        give(azimuth, azimuth, top_re, top_im)
        older, newer = None, (top_re, top_im)
        for degree in range(azimuth + 1, ORDER + 1):
            denom = math.sqrt(degree * degree - azimuth * azimuth)
            scaled = ((2 * degree - 1) / denom) * coord_z
            lower = None
            if degree - 2 >= azimuth:
                lower = (math.sqrt((degree - 1) ** 2 - azimuth * azimuth) / denom) * radius2
            values = []
            for part in range(1 if azimuth == 0 else 2):
                value = scaled * newer[part]
                if lower is not None:
                    value = value - lower * older[part]
                values.append(value)
            older, newer = newer, tuple(values)
            give(degree, azimuth, values[0], values[-1])


def flatten(field, flat):
    size_x, size_y, size_z = field.shape[:3]
    for a in range(size_x):
        for b in range(size_y):
            first = (a * size_y + b) * size_z
            flat[first : first + size_z, :] = field[a, b]


def flatten_children(field, flat, cells):
    _, cells_y, cells_z = cells
    for parent in range(flat.shape[0] // 8):
        for octant in range(0, 8, 2):
            leaf = child_leaf(parent, octant, cells)
            a, b, c = leaf // (cells_y * cells_z), leaf // cells_z % cells_y, leaf % cells_z
            first = 8 * parent + octant
            flat[first : first + 2, :] = field[a, b, c : c + 2]


def fill_basis(offsets, flat, basis):
    leaves = flat.shape[1]
    for axis in range(3):
        flatten(offsets.at[axis], flat.at[axis])
    for first in range(0, leaves, 8):
        fill_rows(flat, basis, first)


def fill_rows(flat, basis, first):
    rows = slice(first, first + 8)
    x, y, z = (flat[axis, rows, :] - 0.5 for axis in range(3))

    def emit(index, value):
        basis[index, rows, :] = value

    emit_harmonics(x, y, z, emit)


def child_leaf(parent, octant, cells):
    _, cells_y, cells_z = cells
    half_y, half_z = cells_y // 2, cells_z // 2
    a = parent // (half_y * half_z)
    b = parent // half_z % half_y
    c = parent % half_z
    x = 2 * a + octant // 4
    y = 2 * b + octant // 2 % 2
    z = 2 * c + octant % 2
    return (x * cells_y + y) * cells_z + z


def limits(counts, first, size, width):
    _, size_y, size_z = counts.shape
    rows = iota((size, width), 0)
    limit = jnp.zeros((size, width), jnp.int32)
    for row in range(size):
        leaf = first + row
        count = counts[leaf // (size_y * size_z), leaf // size_z % size_y, leaf % size_z]
        limit = jnp.where(rows == row, count, limit)
    return limit


def over(value, divisor):
    return jnp.floor((value + 0.5) * (1.0 / divisor))


def columns(cell, halves, peers):
    (half_x, half_y, half_z), (_, count_y, count_z) = halves, peers
    parents_y, parents_z = half_y * count_y, half_z * count_z
    cell_a = over(cell, parents_y * parents_z)
    rest = cell - cell_a * (parents_y * parents_z)
    cell_b = over(rest, parents_z)
    cell_c = rest - cell_b * parents_z
    device, local = 0.0, 0.0
    for part, half, count in zip((cell_a, cell_b, cell_c), halves, peers):
        owner = over(part, half)
        device = device * count + owner
        local = local * half + (part - owner * half)
    return device * (half_x * half_y * half_z) + local


def multipole_body(info, counts, owned, offsets, charges, upward, sources, classes, out, *scratch):
    cells, peers, wide = info
    flat, charge, basis, sums = scratch
    leaves, width = charge.shape
    coef = upward.shape[0]
    per_device = leaves // 8
    halves = tuple(size // 2 for size in cells)
    flatten(charges, charge)
    for first in range(0, leaves, 8):
        live = iota((8, width), 1) < limits(counts, first, 8, width)
        charge[first : first + 8, :] = jnp.where(live, charge[first : first + 8, :], 0.0)
    fill_basis(offsets, flat, basis)
    parts = jnp.concatenate(split3(charge[...]) + (jnp.zeros((128 - 3 * leaves, width)),), 0)
    columns_all = parts.T
    lane = iota((width, 128), 1)
    chunk = next(n for n in range(11, 0, -1) if coef % n == 0)
    rights = [narrow(jnp.where(lane < leaves * (3 - j), columns_all, 0.0)) for j in range(3)]
    keep = iota((chunk, leaves, 128), 1) == iota((chunk, leaves, 128), 2) % leaves
    for start in range(0, coef, chunk):
        lefts = split3(basis[start : start + chunk].reshape(chunk * leaves, width))
        result = sum(multiply(left, right) for left, right in zip(lefts, rights))
        result = jnp.where(keep, result.reshape(chunk, leaves, 128), 0.0)
        sums[start : start + chunk, :] = jnp.sum(result, 1)
    folded = sums[...]
    folded = folded + pltpu.roll(folded, 128 - leaves, 1) + pltpu.roll(folded, 128 - 2 * leaves, 1)
    lane = iota((coef, 128), 1)
    first, second, third = split3(folded)
    stacked = jnp.where(lane < leaves, first, 0.0)
    stacked = jnp.where(lane // leaves == 1, pltpu.roll(second, leaves, 1), stacked)
    stacked = jnp.where(lane // leaves == 2, pltpu.roll(third, 2 * leaves, 1), stacked)
    span = 128 // per_device
    row, col = iota((128, 128), 0), iota((128, 128), 1)
    slot = col % span
    wanted = child_leaf(col // span, slot // 3, cells) + leaves * (slot % 3)
    chosen = multiply(stacked, mask((row == wanted) & (slot < 24)))
    slot = lane % span
    result = jnp.zeros((coef * 8, 128), jnp.float32)
    for j, left in enumerate(split3(upward[...].reshape(coef * 8, coef))):
        result = result + multiply(left, jnp.where(slot % 3 < 3 - j, chosen, 0.0))
    shape = (coef, 8, 128)
    result = jnp.where(iota(shape, 1) == iota(shape, 2) % span // 3, result.reshape(shape), 0.0)
    parent = jnp.sum(jnp.sum(result, 1).T.reshape(per_device, span, coef), 1)

    def wider(value, size):
        fill = jnp.zeros((per_device, size - value.shape[1]), jnp.float32)
        return jnp.concatenate([value, fill], 1)

    shape = (per_device, 128)
    cell = jnp.zeros(shape, jnp.float32)
    for row in range(per_device):
        cell = jnp.where(iota(shape, 0) == row, owned[row].astype(jnp.float32), cell)
    column = columns(cell, halves, peers)
    upper = over(column, 256)
    head = wider(parent, 128)
    head = jnp.where(iota(shape, 1) == coef, column - 256.0 * upper, head)
    head = jnp.where(iota(shape, 1) == coef + 1, upper, head)
    column = columns(sources[...].astype(jnp.float32), halves, peers)
    upper = over(column, 256)
    pieces = [head, wider(classes[...].astype(jnp.float32), 256)]
    pieces.append(wider(column - 256.0 * upper, 256))
    if wide == 3:
        pieces.append(wider(upper, 256))
    payload = narrow(jnp.concatenate(pieces, 1))

    def spread(device, carry):
        out[device] = payload
        return carry

    lax.fori_loop(0, out.shape[0], spread, 0, unroll=8)


def multipole(counts, owned, offsets, charges, upward, sources, classes, peers, wide):
    cells, width = charges.shape[:3], charges.shape[3]
    leaves = cells[0] * cells[1] * cells[2]
    coef = upward.shape[0]
    devices = peers[0] * peers[1] * peers[2]
    smem = pl.BlockSpec(memory_space=pltpu.SMEM)
    vmem = pl.BlockSpec(memory_space=pltpu.VMEM)
    return pl.pallas_call(
        functools.partial(multipole_body, (cells, peers, wide)),
        out_shape=jax.ShapeDtypeStruct((devices, leaves // 8, 128 + 256 * wide), jnp.bfloat16),
        in_specs=[smem, smem] + [vmem] * 5,
        out_specs=vmem,
        scratch_shapes=[
            pltpu.VMEM((3, leaves, width), jnp.float32),
            pltpu.VMEM((leaves, width), jnp.float32),
            pltpu.VMEM((coef, leaves, width), jnp.float32),
            pltpu.VMEM((coef, 128), jnp.float32),
        ],
        name="multipole",
    )(counts, owned, offsets, charges, upward, sources, classes)


FETCHES = 4


def translate_body(info, mine, counts, arrived, remote, offsets, near, downward, out, *scratch):
    cells, per_device, lists, wide = info
    table, matrix, weights, sums, flat, basis, spread_local, sem = scratch
    coef, _, ops = matrix.shape
    chunk = next(n for n in range(11, 0, -1) if coef % n == 0)
    fetches = []
    for start in range(0, coef, chunk):
        window = pl.ds(start, chunk)
        copy = pltpu.make_async_copy(remote.at[window], matrix.at[window], sem.at[start // chunk])
        copy.start()
        fetches.append(copy)
    leaves, width = near.shape
    _, cells_y, cells_z = cells
    rows = table.shape[0]
    span = 128 // per_device
    blocks = -(-coef // span)
    for axis in range(3):
        flatten_children(offsets.at[axis], flat.at[axis], cells)
    group = 8 // per_device

    def settle(index, carry):
        rows = [arrived[index * group + part].astype(jnp.float32) for part in range(group)]
        table[pl.ds(pl.multiple_of(8 * index, 8), 8), :] = jnp.concatenate(rows, 0)
        return carry

    lax.fori_loop(0, arrived.shape[0] // group, settle, 0, unroll=4)

    seg = 256
    head = table[:, 0:128]
    owned = head[:, coef : coef + 1] + 256.0 * head[:, coef + 1 : coef + 2]
    lane = iota((rows, 128), 1)
    chosen = mask((owned.astype(jnp.int32) == lane + mine[0]) & (lane < per_device))
    entries = multiply(chosen.T[0:8], table[:, 128 : 128 + wide * seg])
    sources = entries[:, seg : 2 * seg]
    if wide == 3:
        sources = sources + 256.0 * entries[:, 2 * seg : 3 * seg]
    sources = sources.astype(jnp.int32)
    classes = entries[:, 0:seg].astype(jnp.int32)
    across = (((1,), (1,)), ((), ()))
    counted = []
    fill_rows(flat, basis, 0)
    for row in range(per_device):
        from_cell = mask(iota((rows, seg), 0) == sources[row : row + 1])
        to_class = iota((ops, seg), 0) == classes[row : row + 1]
        to_class = mask(to_class & (iota((ops, seg), 1) < lists))
        counted.append(narrow(multiply(to_class, from_cell, across)))
    counted = jnp.concatenate(counted, 1)
    for first in range(8, leaves - 8, 8):
        fill_rows(flat, basis, first)
    parents = table[:, 0:128]
    for block in range(blocks):
        row, col = iota((128, 128), 0), iota((128, 128), 1)
        tiled = multiply(parents, mask((row == span * block + col % span) & (row < coef)))
        stacked = [jnp.where(lane // span == row, tiled, 0.0) for row in range(per_device)]
        weights[block] = narrow(multiply(counted, jnp.concatenate(stacked, 0)))
    fill_rows(flat, basis, leaves - 8)
    for start in range(0, coef, chunk):
        if start // chunk % FETCHES == 0:
            for copy in fetches[start // chunk : start // chunk + FETCHES]:
                copy.wait()
        total = jnp.zeros((chunk, 128), jnp.float32)
        for block in range(blocks):
            height = min(span, coef - span * block)
            part = matrix[start : start + chunk, span * block : span * block + height, :]
            if height < span:
                fill = jnp.zeros((chunk, span - height, ops), part.dtype)
                part = jnp.concatenate([part, fill], 1)
            result = multiply(part.reshape(chunk * span, ops), weights[block])
            result = result.reshape(chunk, span, 128)
            keep = iota((chunk, span, 128), 1) == iota((chunk, span, 128), 2) % span
            total = total + jnp.sum(jnp.where(keep, result, 0.0), 1)
        sums[start : start + chunk, :] = total
    gather = mask(iota((128, 128), 0) // span == iota((128, 128), 1))
    local = sum(multiply(piece, gather) for piece in split3(sums[...]))
    first, second, _ = split3(local)
    for start in range(0, coef, chunk):
        rows = downward[start : start + chunk].reshape(chunk * 8, coef)
        upper, lower, _ = split3(rows)
        result = multiply(upper, first) + (multiply(upper, second) + multiply(lower, first))
        spread_local[8 * start : 8 * (start + chunk), :] = result
    for parent in range(per_device):
        rows = slice(8 * parent, 8 * parent + 8)
        total = jnp.zeros((8, width), jnp.float32)
        for index in range(coef):
            values = spread_local[8 * index : 8 * index + 8, parent : parent + 1]
            total = total + jnp.broadcast_to(values, (8, width)) * basis[index, rows, :]
        for octant in range(0, 8, 2):
            leaf = child_leaf(parent, octant, cells)
            a, b, c = leaf // (cells_y * cells_z), leaf // cells_z % cells_y, leaf % cells_z
            limit = jnp.zeros((2, width), jnp.int32)
            for row in range(2):
                limit = jnp.where(iota((2, width), 0) == row, counts[a, b, c + row], limit)
            value = total[octant : octant + 2] + near[leaf : leaf + 2, :]
            out[a, b, c : c + 2, :] = jnp.where(iota((2, width), 1) < limit, value, 0.0)


def translate(mine, counts, table, matrix, offsets, near, downward, lists, wide):
    cells = counts.shape
    coef, _, ops = matrix.shape
    leaves, width = near.shape
    per_device = leaves // 8
    span = 128 // per_device
    smem = pl.BlockSpec(memory_space=pltpu.SMEM)
    vmem = pl.BlockSpec(memory_space=pltpu.VMEM)
    return pl.pallas_call(
        functools.partial(translate_body, (cells, per_device, lists, wide)),
        out_shape=jax.ShapeDtypeStruct(cells + (width,), jnp.float32),
        in_specs=[smem, smem, vmem, pl.BlockSpec(memory_space=pl.ANY)] + [vmem] * 3,
        out_specs=vmem,
        scratch_shapes=[
            pltpu.VMEM((table.shape[0] * table.shape[1], table.shape[2]), jnp.float32),
            pltpu.VMEM(matrix.shape, matrix.dtype),
            pltpu.VMEM((-(-coef // span), ops, 128), jnp.bfloat16),
            pltpu.VMEM((coef, 128), jnp.float32),
            pltpu.VMEM((3, leaves, width), jnp.float32),
            pltpu.VMEM((coef, leaves, width), jnp.float32),
            pltpu.VMEM((8 * coef, 128), jnp.float32),
            pltpu.SemaphoreType.DMA((coef,)),
        ],
        compiler_params=pltpu.CompilerParams(vmem_limit_bytes=50 << 20),
        name="translate",
    )(mine, counts, table, matrix, offsets, near, downward)


MESH_AXES = ("gx", "gy", "gz")


def padded_along(value, axis, dim):
    peers, length = lax.axis_size(axis), value.shape[dim]
    last = lax.slice_in_dim(value, length - 1, length, axis=dim)
    leading = lax.slice_in_dim(value, 0, 1, axis=dim)
    if peers == 2:
        upper = lax.axis_index(axis) == 1
        other = lax.ppermute(jnp.where(upper, leading, last), axis, [(0, 1), (1, 0)])
        before = jnp.where(upper, other, 0.0)
        after = jnp.where(upper, 0.0, other)
    else:
        up = [(i, i + 1) for i in range(peers - 1)]
        before = lax.ppermute(last, axis, up)
        after = lax.ppermute(leading, axis, [(j, i) for i, j in up])
    return before, value, after


def per_block(offsets, charges, counts, owned_cell, list_sources, list_ops, m2m, m2l, l2l):
    cells = charges.shape[:3]
    per_device = cells[0] * cells[1] * cells[2] // 8
    peers = tuple(lax.axis_size(axis) for axis in MESH_AXES)
    total_parents = per_device * peers[0] * peers[1] * peers[2]
    sizes = jnp.minimum(counts, charges.shape[3])
    slot_ids = jnp.arange(charges.shape[3], dtype=jnp.int32)
    charge_live = jnp.where(slot_ids[None, None, None, :] < counts[..., None], charges, 0.0)
    padded = jnp.concatenate([offsets, charge_live[None]], 0)
    for axis, dim in (("gz", 3), ("gy", 2)):
        padded = jnp.concatenate(padded_along(padded, axis, dim), dim)
    slabs = padded_along(padded, "gx", 1)

    wide = 2 if total_parents <= 256 else 3
    upward = m2m.transpose(1, 0, 2)
    spread = multipole(
        counts, owned_cell, offsets, charges, upward, list_sources, list_ops, peers, wide
    )
    table = lax.all_to_all(spread, MESH_AXES, 0, 0)

    near = near_field(sizes, slabs, cells)
    mine = (lax.axis_index(MESH_AXES) * per_device).astype(jnp.int32).reshape(1)
    downward = l2l.transpose(1, 0, 2)
    lists = list_sources.shape[1]
    return translate(mine, sizes, table, m2l, offsets, near, downward, lists, wide)


def solution(mesh):
    placed = (
        P(None, "gx", "gy", "gz", None),
        P("gx", "gy", "gz", None),
        P("gx", "gy", "gz"),
        P(("gx", "gy", "gz")),
        P(("gx", "gy", "gz"), None),
        P(("gx", "gy", "gz"), None),
        P(),
        P(),
        P(),
    )
    return jax.shard_map(
        per_block, mesh=mesh, in_specs=placed, out_specs=P("gx", "gy", "gz", None), check_vma=False
    )
```

```python
import math
import functools
import numpy as np
import jax
import jax.numpy as jnp
from jax import lax
from jax.experimental import pallas as pl
from jax.experimental.pallas import tpu as pltpu
from jax.sharding import PartitionSpec as P


ORDER = 10
SOFTENING = 0.01
DELTAS = [(dx, dy, dz) for dx in (-1, 0, 1) for dy in (-1, 0, 1) for dz in (-1, 0, 1)]
DEPTH = 80


def delta_rows(delta):
    row = iota((32, 128), 0)
    values = jnp.zeros((32, 128), jnp.float32)
    for axis in range(3):
        values = jnp.where((row < 9) & (row % 3 == axis), 2.0 * delta[axis], values)
        values = jnp.where((row >= 16) & (row < 25) & (row % 3 == (axis + 1) % 3), delta[axis], values)
    rest = np.float32(sum(d * d for d in delta) + SOFTENING)
    for part in range(3):
        piece = np.asarray(rest).astype(jnp.bfloat16).astype(np.float32)
        values = jnp.where(row == 25 + part, float(piece), values)
        rest = np.float32(rest - piece)
    return values


def expand_rows():
    row, col = iota((32, 128), 0), iota((32, 128), 1)
    slot = col % 16
    triple, axis = slot // 3, slot % 3
    field = col // 16
    known = slot < 9
    product = (field < 3) & known & (triple < 3 - field) & (row == 3 * field + axis)
    offset = (field == 4) & known & (row == slot)
    plain = (field == 0) & (slot >= 9) & (slot < 12) & (row == 12)
    norm = (field == 0) & (slot >= 12) & (slot < 15) & (row == slot - 3)
    shift = (field == 3) & known & (row == 12)
    rest = (field == 4) & (slot >= 9) & (slot < 12) & (row == 12)
    values = jnp.where(product | offset, -2.0, 0.0)
    return jnp.where(plain | norm | shift | rest, 1.0, values)


def split3(value):
    first = value.astype(jnp.bfloat16).astype(jnp.float32)
    rest = value - first
    second = rest.astype(jnp.bfloat16).astype(jnp.float32)
    third = (rest - second).astype(jnp.bfloat16).astype(jnp.float32)
    return first, second, third


def iota(shape, dim):
    return lax.broadcasted_iota(jnp.int32, shape, dim)


def mask(condition):
    return jnp.where(condition, 1.0, 0.0)


def narrow(value):
    return value.astype(jnp.bfloat16)


def multiply(left, right, dims=(((1,), (0,)), ((), ()))):
    return lax.dot_general(narrow(left), narrow(right), dims, preferred_element_type=jnp.float32)


def near_body(cells, counts, lower, middle, upper, out, rows32, base, left, total, table):
    cells_x, cells_y, cells_z = cells
    _, _, pad_y, pad_z, width = middle.shape
    pad_x = cells_x + 2
    leaves = cells_x * cells_y * cells_z
    tiles = width // 128
    sources = pad_x * pad_y * pad_z

    def fill(source, first, place, carry):
        a, b = place // pad_y, place % pad_y
        column = first * pad_y + place
        parts, norm = [], 0.0
        for axis in range(3):
            centred = source[axis, a, b] - 0.5
            norm = norm + centred * centred
            parts.append(split3(centred))
        rows = [parts[axis][part] for part in range(3) for axis in range(3)]
        rows += list(split3(norm)) + [jnp.ones_like(norm)] * 3 + [source[3, a, b]]
        for index, row in enumerate(rows):
            for part in range(tiles):
                start = part * sources * 16 + column * pad_z * 16 + index
                rows32[pl.ds(start, pad_z, stride=16), :] = row[:, 128 * part : 128 * part + 128]
        return carry

    def pack(leaf, carry):
        for part in range(tiles):
            start = pl.multiple_of((part * sources + leaf) * 16, 16)
            base[leaf, :, 128 * part : 128 * part + 128] = narrow(rows32[pl.ds(start, 16), :])
        return carry

    for index, delta in enumerate(DELTAS):
        table[index] = narrow(delta_rows(delta))
    table[len(DELTAS)] = narrow(expand_rows())
    for source, first in ((lower, 0), (middle, 1), (upper, cells_x + 1)):
        columns = source.shape[1] * pad_y
        lax.fori_loop(0, columns, functools.partial(fill, source, first), 0, unroll=2)
    lax.fori_loop(0, pad_x * pad_y * pad_z, pack, 0, unroll=8)

    def place(leaf):
        return leaf // (cells_y * cells_z), leaf // cells_z % cells_y, leaf % cells_z

    def home(leaf):
        a, b, c = place(leaf)
        return ((a + 1) * pad_y + b + 1) * pad_z + c + 1

    def count_of(leaf):
        a, b, c = place(leaf)
        return counts[a, b, c]

    def fill_left(leaf):
        features = base[home(leaf)].astype(jnp.float32).T
        left[leaf % 2] = narrow(multiply(features, table[len(DELTAS), 0:16]))

    ones = jnp.ones((8, 128), jnp.bfloat16)
    across = (((1,), (1,)), ((), ()))

    def finish(leaf):
        result = sum(multiply(ones, piece, across) for piece in split3(total[leaf % 2]))
        slot = iota((1, width), 1)
        out[pl.ds(leaf, 1), :] = jnp.where(slot < count_of(leaf), result[0:1], 0.0)

    def block(leaf, height):
        centre = home(leaf)
        lhs = left[leaf % 2, 0:height, 0:DEPTH]
        acc = jnp.zeros((height, 128), jnp.float32)
        for index, (dx, dy, dz) in enumerate(DELTAS):
            other = centre + (dx * pad_y + dy) * pad_z + dz
            scale = table[index, 0:16]
            fixed = table[index, 16:32]
            halves = []
            for part in range(tiles):
                feature = base[other, :, 128 * part : 128 * part + 128]
                halves.append(
                    jnp.concatenate([feature, feature, feature, feature * scale, fixed], 0)
                )
            rhs = jnp.concatenate(halves, 1)
            dist2 = jnp.dot(lhs, rhs, preferred_element_type=jnp.float32)
            inverse = lax.rsqrt(dist2)
            if dx == 0 and dy == 0 and dz == 0:
                inverse = jnp.where(iota(inverse.shape, 0) == iota(inverse.shape, 1), 0.0, inverse)
            for part in range(tiles):
                amount = rows32[pl.ds((part * sources + other) * 16 + 15, 1), :]
                acc = acc + inverse[:, 128 * part : 128 * part + 128] * amount
        fill_left(jnp.minimum(leaf + 1, leaves - 1))
        finish(jnp.maximum(leaf - 1, 0))
        total[leaf % 2, 0:height] = acc

    fill_left(0)
    total[...] = jnp.zeros_like(total)
    step = 16

    def choose(leaf, pieces, low, high):
        if high - low == 1:
            block(leaf, high * step)
            return
        middle = (low + high) // 2
        pl.when(pieces <= middle)(lambda: choose(leaf, pieces, low, middle))
        pl.when(pieces > middle)(lambda: choose(leaf, pieces, middle, high))

    def leaf_step(leaf, carry):
        pieces = (count_of(leaf) + step - 1) // step
        choose(leaf, pieces, 0, width // step)
        return carry

    lax.fori_loop(0, leaves, leaf_step, 0)
    finish(leaves - 1)


def near_field(counts, slabs, cells):
    leaves = cells[0] * cells[1] * cells[2]
    width = slabs[1].shape[-1]
    sources = (cells[0] + 2) * slabs[1].shape[2] * slabs[1].shape[3]
    vmem = pl.BlockSpec(memory_space=pltpu.VMEM)
    return pl.pallas_call(
        functools.partial(near_body, cells),
        out_shape=jax.ShapeDtypeStruct((leaves, width), jnp.float32),
        in_specs=[pl.BlockSpec(memory_space=pltpu.SMEM)] + [vmem] * 3,
        out_specs=vmem,
        scratch_shapes=[
            pltpu.VMEM((sources * 16 * (width // 128), 128), jnp.float32),
            pltpu.VMEM((sources, 16, width), jnp.bfloat16),
            pltpu.VMEM((2, width, 128), jnp.bfloat16),
            pltpu.VMEM((2, width, 128), jnp.float32),
            pltpu.VMEM((len(DELTAS) + 1, 32, 128), jnp.bfloat16),
        ],
        cost_estimate=pl.CostEstimate(
            flops=leaves * 27 * width * width * 2 * DEPTH,
            transcendentals=leaves * 27 * width * width,
            bytes_accessed=sources * 4 * width * 4,
        ),
        compiler_params=pltpu.CompilerParams(vmem_limit_bytes=24 << 20),
        name="near",
    )(counts, *slabs)


def emit_harmonics(coord_x, coord_y, coord_z, emit):
    radius2 = coord_x * coord_x + coord_y * coord_y + coord_z * coord_z

    def give(degree, azimuth, real, imag):
        if azimuth == 0:
            emit(degree * degree, real)
        else:
            emit(degree * degree + 2 * azimuth - 1, real)
            emit(degree * degree + 2 * azimuth, imag)

    top_re, top_im = jnp.ones_like(coord_x), None
    for azimuth in range(ORDER + 1):
        if azimuth == 1:
            top_re, top_im = coord_x, coord_y
        elif azimuth > 1:
            factor = math.sqrt((2 * azimuth - 1) / (2 * azimuth))
            top_re, top_im = (
                factor * (coord_x * top_re - coord_y * top_im),
                factor * (coord_x * top_im + coord_y * top_re),
            )
        give(azimuth, azimuth, top_re, top_im)
        older, newer = None, (top_re, top_im)
        for degree in range(azimuth + 1, ORDER + 1):
            denom = math.sqrt(degree * degree - azimuth * azimuth)
            scaled = ((2 * degree - 1) / denom) * coord_z
            lower = None
            if degree - 2 >= azimuth:
                lower = (math.sqrt((degree - 1) ** 2 - azimuth * azimuth) / denom) * radius2
            values = []
            for part in range(1 if azimuth == 0 else 2):
                value = scaled * newer[part]
                if lower is not None:
                    value = value - lower * older[part]
                values.append(value)
            older, newer = newer, tuple(values)
            give(degree, azimuth, values[0], values[-1])


def flatten(field, flat):
    size_x, size_y, size_z = field.shape[:3]
    for a in range(size_x):
        for b in range(size_y):
            first = (a * size_y + b) * size_z
            flat[first : first + size_z, :] = field[a, b]


def flatten_children(field, flat, cells):
    _, cells_y, cells_z = cells
    for parent in range(flat.shape[0] // 8):
        for octant in range(0, 8, 2):
            leaf = child_leaf(parent, octant, cells)
            a, b, c = leaf // (cells_y * cells_z), leaf // cells_z % cells_y, leaf % cells_z
            first = 8 * parent + octant
            flat[first : first + 2, :] = field[a, b, c : c + 2]


def fill_basis(offsets, flat, basis, cells=None):
    leaves = flat.shape[1]
    for axis in range(3):
        if cells:
            flatten_children(offsets.at[axis], flat.at[axis], cells)
        else:
            flatten(offsets.at[axis], flat.at[axis])
    for first in range(0, leaves, 8):
        rows = slice(first, first + 8)
        x, y, z = (flat[axis, rows, :] - 0.5 for axis in range(3))

        def emit(index, value):
            basis[index, rows, :] = value

        emit_harmonics(x, y, z, emit)


def child_leaf(parent, octant, cells):
    _, cells_y, cells_z = cells
    half_y, half_z = cells_y // 2, cells_z // 2
    a = parent // (half_y * half_z)
    b = parent // half_z % half_y
    c = parent % half_z
    x = 2 * a + octant // 4
    y = 2 * b + octant // 2 % 2
    z = 2 * c + octant % 2
    return (x * cells_y + y) * cells_z + z


def limits(counts, first, size, width):
    _, size_y, size_z = counts.shape
    rows = iota((size, width), 0)
    limit = jnp.zeros((size, width), jnp.int32)
    for row in range(size):
        leaf = first + row
        count = counts[leaf // (size_y * size_z), leaf // size_z % size_y, leaf % size_z]
        limit = jnp.where(rows == row, count, limit)
    return limit


def over(value, divisor):
    return jnp.floor((value + 0.5) * (1.0 / divisor))


def columns(cell, halves, peers):
    (half_x, half_y, half_z), (_, count_y, count_z) = halves, peers
    parents_y, parents_z = half_y * count_y, half_z * count_z
    cell_a = over(cell, parents_y * parents_z)
    rest = cell - cell_a * (parents_y * parents_z)
    cell_b = over(rest, parents_z)
    cell_c = rest - cell_b * parents_z
    device, local = 0.0, 0.0
    for part, half, count in zip((cell_a, cell_b, cell_c), halves, peers):
        owner = over(part, half)
        device = device * count + owner
        local = local * half + (part - owner * half)
    return device * (half_x * half_y * half_z) + local


def multipole_body(info, counts, owned, offsets, charges, upward, sources, classes, out, *scratch):
    cells, peers, wide = info
    flat, charge, basis, sums = scratch
    leaves, width = charge.shape
    coef = upward.shape[0]
    per_device = leaves // 8
    halves = tuple(size // 2 for size in cells)
    flatten(charges, charge)
    for first in range(0, leaves, 8):
        live = iota((8, width), 1) < limits(counts, first, 8, width)
        charge[first : first + 8, :] = jnp.where(live, charge[first : first + 8, :], 0.0)
    fill_basis(offsets, flat, basis)
    parts = jnp.concatenate(split3(charge[...]) + (jnp.zeros((128 - 3 * leaves, width)),), 0)
    columns_all = parts.T
    lane = iota((width, 128), 1)
    chunk = next(n for n in range(11, 0, -1) if coef % n == 0)
    rights = [narrow(jnp.where(lane < leaves * (3 - j), columns_all, 0.0)) for j in range(3)]
    keep = iota((chunk, leaves, 128), 1) == iota((chunk, leaves, 128), 2) % leaves
    for start in range(0, coef, chunk):
        lefts = split3(basis[start : start + chunk].reshape(chunk * leaves, width))
        result = sum(multiply(left, right) for left, right in zip(lefts, rights))
        result = jnp.where(keep, result.reshape(chunk, leaves, 128), 0.0)
        sums[start : start + chunk, :] = jnp.sum(result, 1)
    folded = sums[...]
    folded = folded + pltpu.roll(folded, 128 - leaves, 1) + pltpu.roll(folded, 128 - 2 * leaves, 1)
    lane = iota((coef, 128), 1)
    first, second, third = split3(folded)
    stacked = jnp.where(lane < leaves, first, 0.0)
    stacked = jnp.where(lane // leaves == 1, pltpu.roll(second, leaves, 1), stacked)
    stacked = jnp.where(lane // leaves == 2, pltpu.roll(third, 2 * leaves, 1), stacked)
    span = 128 // per_device
    row, col = iota((128, 128), 0), iota((128, 128), 1)
    slot = col % span
    wanted = child_leaf(col // span, slot // 3, cells) + leaves * (slot % 3)
    chosen = multiply(stacked, mask((row == wanted) & (slot < 24)))
    slot = lane % span
    result = jnp.zeros((coef * 8, 128), jnp.float32)
    for j, left in enumerate(split3(upward[...].reshape(coef * 8, coef))):
        result = result + multiply(left, jnp.where(slot % 3 < 3 - j, chosen, 0.0))
    shape = (coef, 8, 128)
    result = jnp.where(iota(shape, 1) == iota(shape, 2) % span // 3, result.reshape(shape), 0.0)
    parent = jnp.sum(jnp.sum(result, 1).T.reshape(per_device, span, coef), 1)

    def wider(value, size):
        fill = jnp.zeros((per_device, size - value.shape[1]), jnp.float32)
        return jnp.concatenate([value, fill], 1)

    shape = (per_device, 128)
    cell = jnp.zeros(shape, jnp.float32)
    for row in range(per_device):
        cell = jnp.where(iota(shape, 0) == row, owned[row].astype(jnp.float32), cell)
    column = columns(cell, halves, peers)
    upper = over(column, 256)
    head = wider(parent, 128)
    head = jnp.where(iota(shape, 1) == coef, column - 256.0 * upper, head)
    head = jnp.where(iota(shape, 1) == coef + 1, upper, head)
    column = columns(sources[...].astype(jnp.float32), halves, peers)
    upper = over(column, 256)
    pieces = [head, wider(classes[...].astype(jnp.float32), 256)]
    pieces.append(wider(column - 256.0 * upper, 256))
    if wide == 3:
        pieces.append(wider(upper, 256))
    payload = narrow(jnp.concatenate(pieces, 1))

    def spread(device, carry):
        out[device] = payload
        return carry

    lax.fori_loop(0, out.shape[0], spread, 0, unroll=8)


def multipole(counts, owned, offsets, charges, upward, sources, classes, peers, wide):
    cells, width = charges.shape[:3], charges.shape[3]
    leaves = cells[0] * cells[1] * cells[2]
    coef = upward.shape[0]
    devices = peers[0] * peers[1] * peers[2]
    smem = pl.BlockSpec(memory_space=pltpu.SMEM)
    vmem = pl.BlockSpec(memory_space=pltpu.VMEM)
    return pl.pallas_call(
        functools.partial(multipole_body, (cells, peers, wide)),
        out_shape=jax.ShapeDtypeStruct((devices, leaves // 8, 128 + 256 * wide), jnp.bfloat16),
        in_specs=[smem, smem] + [vmem] * 5,
        out_specs=vmem,
        scratch_shapes=[
            pltpu.VMEM((3, leaves, width), jnp.float32),
            pltpu.VMEM((leaves, width), jnp.float32),
            pltpu.VMEM((coef, leaves, width), jnp.float32),
            pltpu.VMEM((coef, 128), jnp.float32),
        ],
        name="multipole",
    )(counts, owned, offsets, charges, upward, sources, classes)


FETCHES = 4


def translate_body(info, mine, counts, arrived, remote, offsets, near, downward, out, *scratch):
    cells, per_device, lists, wide = info
    table, matrix, weights, sums, flat, basis, spread_local, sem = scratch
    coef, _, ops = matrix.shape
    chunk = next(n for n in range(11, 0, -1) if coef % n == 0)
    fetches = []
    for start in range(0, coef, chunk):
        window = pl.ds(start, chunk)
        copy = pltpu.make_async_copy(remote.at[window], matrix.at[window], sem.at[start // chunk])
        copy.start()
        fetches.append(copy)
    _, width = near.shape
    _, cells_y, cells_z = cells
    rows = table.shape[0]
    span = 128 // per_device
    blocks = -(-coef // span)
    fill_basis(offsets, flat, basis, cells)
    group = 8 // per_device

    def settle(index, carry):
        rows = [arrived[index * group + part].astype(jnp.float32) for part in range(group)]
        table[pl.ds(pl.multiple_of(8 * index, 8), 8), :] = jnp.concatenate(rows, 0)
        return carry

    lax.fori_loop(0, arrived.shape[0] // group, settle, 0, unroll=4)

    seg = 256
    head = table[:, 0:128]
    owned = head[:, coef : coef + 1] + 256.0 * head[:, coef + 1 : coef + 2]
    lane = iota((rows, 128), 1)
    chosen = mask((owned.astype(jnp.int32) == lane + mine[0]) & (lane < per_device))
    entries = multiply(chosen.T[0:8], table[:, 128 : 128 + wide * seg])
    sources = entries[:, seg : 2 * seg]
    if wide == 3:
        sources = sources + 256.0 * entries[:, 2 * seg : 3 * seg]
    sources = sources.astype(jnp.int32)
    classes = entries[:, 0:seg].astype(jnp.int32)
    across = (((1,), (1,)), ((), ()))
    counted = []
    for row in range(per_device):
        from_cell = mask(iota((rows, seg), 0) == sources[row : row + 1])
        to_class = iota((ops, seg), 0) == classes[row : row + 1]
        to_class = mask(to_class & (iota((ops, seg), 1) < lists))
        counted.append(narrow(multiply(to_class, from_cell, across)))
    counted = jnp.concatenate(counted, 1)
    parents = table[:, 0:128]
    for block in range(blocks):
        row, col = iota((128, 128), 0), iota((128, 128), 1)
        tiled = multiply(parents, mask((row == span * block + col % span) & (row < coef)))
        stacked = [jnp.where(lane // span == row, tiled, 0.0) for row in range(per_device)]
        weights[block] = narrow(multiply(counted, jnp.concatenate(stacked, 0)))
    for start in range(0, coef, chunk):
        if start // chunk % FETCHES == 0:
            for copy in fetches[start // chunk : start // chunk + FETCHES]:
                copy.wait()
        total = jnp.zeros((chunk, 128), jnp.float32)
        for block in range(blocks):
            height = min(span, coef - span * block)
            part = matrix[start : start + chunk, span * block : span * block + height, :]
            if height < span:
                fill = jnp.zeros((chunk, span - height, ops), part.dtype)
                part = jnp.concatenate([part, fill], 1)
            result = multiply(part.reshape(chunk * span, ops), weights[block])
            result = result.reshape(chunk, span, 128)
            keep = iota((chunk, span, 128), 1) == iota((chunk, span, 128), 2) % span
            total = total + jnp.sum(jnp.where(keep, result, 0.0), 1)
        sums[start : start + chunk, :] = total
    gather = mask(iota((128, 128), 0) // span == iota((128, 128), 1))
    local = sum(multiply(piece, gather) for piece in split3(sums[...]))
    first, second, _ = split3(local)
    for start in range(0, coef, chunk):
        rows = downward[start : start + chunk].reshape(chunk * 8, coef)
        upper, lower, _ = split3(rows)
        result = multiply(upper, first) + (multiply(upper, second) + multiply(lower, first))
        spread_local[8 * start : 8 * (start + chunk), :] = result
    for parent in range(per_device):
        rows = slice(8 * parent, 8 * parent + 8)
        total = jnp.zeros((8, width), jnp.float32)
        for index in range(coef):
            values = spread_local[8 * index : 8 * index + 8, parent : parent + 1]
            total = total + jnp.broadcast_to(values, (8, width)) * basis[index, rows, :]
        for octant in range(0, 8, 2):
            leaf = child_leaf(parent, octant, cells)
            a, b, c = leaf // (cells_y * cells_z), leaf // cells_z % cells_y, leaf % cells_z
            limit = jnp.zeros((2, width), jnp.int32)
            for row in range(2):
                limit = jnp.where(iota((2, width), 0) == row, counts[a, b, c + row], limit)
            value = total[octant : octant + 2] + near[leaf : leaf + 2, :]
            out[a, b, c : c + 2, :] = jnp.where(iota((2, width), 1) < limit, value, 0.0)


def translate(mine, counts, table, matrix, offsets, near, downward, lists, wide):
    cells = counts.shape
    coef, _, ops = matrix.shape
    leaves, width = near.shape
    per_device = leaves // 8
    span = 128 // per_device
    smem = pl.BlockSpec(memory_space=pltpu.SMEM)
    vmem = pl.BlockSpec(memory_space=pltpu.VMEM)
    return pl.pallas_call(
        functools.partial(translate_body, (cells, per_device, lists, wide)),
        out_shape=jax.ShapeDtypeStruct(cells + (width,), jnp.float32),
        in_specs=[smem, smem, vmem, pl.BlockSpec(memory_space=pl.ANY)] + [vmem] * 3,
        out_specs=vmem,
        scratch_shapes=[
            pltpu.VMEM((table.shape[0] * table.shape[1], table.shape[2]), jnp.float32),
            pltpu.VMEM(matrix.shape, matrix.dtype),
            pltpu.VMEM((-(-coef // span), ops, 128), jnp.bfloat16),
            pltpu.VMEM((coef, 128), jnp.float32),
            pltpu.VMEM((3, leaves, width), jnp.float32),
            pltpu.VMEM((coef, leaves, width), jnp.float32),
            pltpu.VMEM((8 * coef, 128), jnp.float32),
            pltpu.SemaphoreType.DMA((coef,)),
        ],
        compiler_params=pltpu.CompilerParams(vmem_limit_bytes=50 << 20),
        name="translate",
    )(mine, counts, table, matrix, offsets, near, downward)


MESH_AXES = ("gx", "gy", "gz")


def padded_along(value, axis, dim):
    peers, length = lax.axis_size(axis), value.shape[dim]
    last = lax.slice_in_dim(value, length - 1, length, axis=dim)
    leading = lax.slice_in_dim(value, 0, 1, axis=dim)
    if peers == 2:
        upper = lax.axis_index(axis) == 1
        other = lax.ppermute(jnp.where(upper, leading, last), axis, [(0, 1), (1, 0)])
        before = jnp.where(upper, other, 0.0)
        after = jnp.where(upper, 0.0, other)
    else:
        up = [(i, i + 1) for i in range(peers - 1)]
        before = lax.ppermute(last, axis, up)
        after = lax.ppermute(leading, axis, [(j, i) for i, j in up])
    return before, value, after


def per_block(offsets, charges, counts, owned_cell, list_sources, list_ops, m2m, m2l, l2l):
    cells = charges.shape[:3]
    per_device = cells[0] * cells[1] * cells[2] // 8
    peers = tuple(lax.axis_size(axis) for axis in MESH_AXES)
    total_parents = per_device * peers[0] * peers[1] * peers[2]
    sizes = jnp.minimum(counts, charges.shape[3])
    slot_ids = jnp.arange(charges.shape[3], dtype=jnp.int32)
    charge_live = jnp.where(slot_ids[None, None, None, :] < counts[..., None], charges, 0.0)
    padded = jnp.concatenate([offsets, charge_live[None]], 0)
    for axis, dim in (("gz", 3), ("gy", 2)):
        padded = jnp.concatenate(padded_along(padded, axis, dim), dim)
    slabs = padded_along(padded, "gx", 1)

    wide = 2 if total_parents <= 256 else 3
    upward = m2m.transpose(1, 0, 2)
    spread = multipole(
        counts, owned_cell, offsets, charges, upward, list_sources, list_ops, peers, wide
    )
    table = lax.all_to_all(spread, MESH_AXES, 0, 0)

    near = near_field(sizes, slabs, cells)
    mine = (lax.axis_index(MESH_AXES) * per_device).astype(jnp.int32).reshape(1)
    downward = l2l.transpose(1, 0, 2)
    lists = list_sources.shape[1]
    return translate(mine, sizes, table, m2l, offsets, near, downward, lists, wide)


def solution(mesh):
    placed = (
        P(None, "gx", "gy", "gz", None),
        P("gx", "gy", "gz", None),
        P("gx", "gy", "gz"),
        P(("gx", "gy", "gz")),
        P(("gx", "gy", "gz"), None),
        P(("gx", "gy", "gz"), None),
        P(),
        P(),
        P(),
    )
    return jax.shard_map(
        per_block, mesh=mesh, in_specs=placed, out_specs=P("gx", "gy", "gz", None), check_vma=False
    )
```
